256 devices in a mesh: row: 8 (over z), col: 32 (over y, x, core).
Axes of the slice: x: 4, y: 4, z: 8, core: 2. Of those that a mesh axis runs over, the one named last changes fastest.
Arguments:
- matrix: float32 [16384, 16384], P('row', 'col'), may hold values from -48 to 48, as said below
- pivots: int32 [2, 64], replicated, may hold values from 128 to 16383, as said below
Outputs:
- factored: float32 [16384, 16384], P('row', 'col')
The draws below stay inside these ranges and needn't reach their ends.
Inputs may be any that keep to these rules, and one draw needn't show every extreme that they name: `pivots`: the 128 entries are distinct global row numbers. `matrix`: the entry of row pivots[c, k] in global column c * 64 + k dominates the other entries of its global column, so that multipliers stay well below one.
All inputs are finite; a program needn't handle non-finite values.
Results may differ from the reference program's by a relative error of at most 0.0002.
Values sent between devices are 32-bit elements; how exact they have to be, the bound alone decides.
A program may use at most 64 MiB of HBM per device.

```python
import math
import jax
import jax.numpy as jnp
from jax import lax

NB = 64
ORDER = 16384
BLK_ROWS = 32
BLK_COLS = 8
N_ROW = 8
N_COL = 32


def pivot_rows(key):
    sub_key = jax.random.fold_in(key, 11)
    chosen = jax.random.permutation(sub_key, ORDER - 2 * NB)[:2 * NB] + 2 * NB
    return chosen.astype(jnp.int32)


def draw_pivots(key, part):
    return pivot_rows(key).reshape(2, NB)


def draw_matrix(key, part):
    grid_rows = ORDER // (NB * BLK_ROWS)
    grid_cols = ORDER // (NB * BLK_COLS)
    key_values = jax.random.fold_in(key, 21)
    key_sizes = jax.random.fold_in(key, 23)
    key_signs = jax.random.fold_in(key, 24)
    values = 0.4 * jax.random.truncated_normal(key_values, -4.0, 4.0, (ORDER, ORDER), jnp.float32)
    chosen = pivot_rows(key)
    magnitudes = jnp.exp(jax.random.uniform(key_sizes, (2 * NB,), jnp.float32, math.log(16.0), math.log(48.0)))
    sign_values = jnp.where(jax.random.bernoulli(key_signs, 0.5, (2 * NB,)), 1.0, -1.0)
    values = values.at[chosen, jnp.arange(2 * NB)].set(magnitudes * sign_values)
    values = values.reshape(BLK_ROWS, grid_rows, NB, BLK_COLS, grid_cols, NB)
    return values.transpose(1, 0, 2, 4, 3, 5).reshape(ORDER, ORDER)


def setup_inputs(seed: int = 0) -> dict:
    seeds = jax.random.split(jax.random.key(seed), 3)
    return {
        "matrix": draw_matrix(jax.random.fold_in(seeds[2], 71), 0),
        "pivots": draw_pivots(jax.random.fold_in(seeds[2], 71), 0),
    }


HIGHEST_PRECISION = lax.Precision.HIGHEST

def eliminate(panel_t):
    panel_width, row_count = panel_t.shape
    row_ids = jnp.arange(row_count, dtype=jnp.int32)
    col_ids = jnp.arange(panel_width, dtype=jnp.int32)

    def eliminate_step(column, current):
        pivot_line = lax.dynamic_index_in_dim(current, column, 1, keepdims=False)
        pivot_value = lax.dynamic_index_in_dim(pivot_line, column, 0, keepdims=False)
        weight = 1.0 / pivot_value
        column_line = lax.dynamic_index_in_dim(current, column, 0, keepdims=False)
        below_rows = row_ids > column
        multiplier = jnp.where(below_rows, column_line * weight, 0.0)
        later_part = jnp.where(col_ids > column, pivot_line, 0.0)
        current = current - later_part[:, None] * multiplier[None, :]
        return jnp.where((col_ids == column)[:, None] & below_rows[None, :], multiplier[None, :], current)
    return lax.fori_loop(0, panel_width, eliminate_step, panel_t)

def solve_rows(top_t, right_side):
    unit_part = jnp.tril(top_t.T, -1) + jnp.eye(top_t.shape[0], dtype=top_t.dtype)
    return lax.linalg.triangular_solve(unit_part, right_side, left_side=True, lower=True, unit_diagonal=True)

def reference(matrix, pivots):
    grid_rows = N_ROW
    grid_cols = N_COL
    whole_matrix = matrix.reshape(grid_rows, BLK_ROWS, NB, grid_cols, BLK_COLS, NB)
    whole_matrix = whole_matrix.transpose(1, 0, 2, 4, 3, 5).reshape(ORDER, ORDER)
    top_global = jnp.arange(2 * NB, dtype=jnp.int32)
    pivot_global = pivots.reshape(-1).astype(jnp.int32)
    order_index = jnp.arange(ORDER, dtype=jnp.int32).at[top_global].set(pivot_global).at[pivot_global].set(top_global)
    whole_matrix = whole_matrix[order_index]
    for panel in range(2):
        first_row = panel * NB
        factored_panel = eliminate(whole_matrix[first_row:, first_row:first_row + NB].T)
        whole_matrix = whole_matrix.at[first_row:, first_row:first_row + NB].set(factored_panel.T)
        upper_rows = solve_rows(factored_panel[:, :NB], whole_matrix[first_row:first_row + NB, first_row + NB:])
        whole_matrix = whole_matrix.at[first_row:first_row + NB, first_row + NB:].set(upper_rows)
        product = lax.dot_general(factored_panel[:, NB:].astype(jnp.float32), upper_rows.astype(jnp.float32), (((0,), (0,)), ((), ())), precision=HIGHEST_PRECISION, preferred_element_type=jnp.float32)
        whole_matrix = whole_matrix.at[first_row + NB:, first_row + NB:].set(whole_matrix[first_row + NB:, first_row + NB:] - product)
    result = whole_matrix.reshape(BLK_ROWS, grid_rows, NB, BLK_COLS, grid_cols, NB)
    return result.transpose(1, 0, 2, 4, 3, 5).reshape(ORDER, ORDER)
```

```python
import jax
import jax.numpy as jnp
from jax import lax
from jax.experimental import pallas as pl
from jax.experimental.pallas import tpu as pltpu
from jax.sharding import PartitionSpec as P

NB = 64
TOP = 2 * NB
SUB = 8
CHUNKS = 8
HIGHEST = lax.Precision.HIGHEST


def dot(a, b):
    return lax.dot_general(
        a, b, (((1,), (0,)), ((), ())), precision=HIGHEST, preferred_element_type=jnp.float32
    )


def factor(a_ref, lu_ref, linv_ref, uinv_ref):
    n = TOP // SUB
    lane = lax.broadcasted_iota(jnp.int32, (SUB, TOP), 1)
    sub = lax.broadcasted_iota(jnp.int32, (SUB, TOP), 0)
    a = [a_ref[SUB * i : SUB * (i + 1), :] for i in range(n)]
    eye = [jnp.where(lane == sub + SUB * i, 1.0, 0.0).astype(jnp.float32) for i in range(n)]
    low = list(eye)
    upp = list(eye)
    weights = jnp.ones((SUB, TOP), jnp.float32)
    for k in range(TOP):
        kb, ks = divmod(k, SUB)
        row = jnp.broadcast_to(a[kb][ks : ks + 1, :], (SUB, TOP))
        low_row = jnp.broadcast_to(low[kb][ks : ks + 1, :], (SUB, TOP))
        weight = 1.0 / jnp.broadcast_to(row[:, k : k + 1], (SUB, TOP))
        weights = jnp.where(lane == k, weight, weights)
        scaled = jnp.where(lane > k, row * weight, 0.0)
        low_scaled = low_row * weight
        for i in range(kb, n):
            column = jnp.broadcast_to(a[i][:, k : k + 1], (SUB, TOP))
            if i == kb:
                column = jnp.where(sub > ks, column, 0.0)
            a[i] = a[i] - column * scaled
            low[i] = low[i] - column * low_scaled
        for i in range(kb + 1):
            column = jnp.broadcast_to(upp[i][:, k : k + 1], (SUB, TOP))
            upp[i] = upp[i] - column * scaled
    for i in range(n):
        part = slice(SUB * i, SUB * (i + 1))
        lu_ref[part, :] = jnp.where(sub + SUB * i > lane, a[i] * weights, a[i])
        linv_ref[part, :] = low[i]
        uinv_ref[part, :] = upp[i] * weights


def finish_kernel(
    where_ref,
    a_ref,
    panel_ref,
    lead_ref,
    new_top_ref,
    old_top_ref,
    old_lead_ref,
    out_ref,
    a_buf,
    p_buf,
    lu,
    linv,
    uinv,
    in_sem,
    panel_sem,
    out_sem,
):
    my_row = lax.axis_index("row")
    my_col = lax.axis_index("col")
    rows = a_buf.shape[0] // CHUNKS
    copies = [
        pltpu.make_async_copy(
            a_ref.at[pl.ds(rows * i, rows)], a_buf.at[pl.ds(rows * i, rows)], in_sem.at[i]
        )
        for i in range(CHUNKS)
    ]
    panel_copy = pltpu.make_async_copy(panel_ref, p_buf, panel_sem)
    panel_copy.start()
    for copy in copies:
        copy.start()
    factor(lead_ref, lu, linv, uinv)
    cols = a_buf.shape[1]
    upper = dot(linv[...], new_top_ref[...])
    solved = dot(uinv[...], upper)
    holds = my_col < 2
    first_cols = lax.broadcasted_iota(jnp.int32, (TOP, cols), 1) < NB
    own = jnp.where(my_col == 0, uinv[:, :NB], uinv[:, NB:])
    own = jnp.concatenate([own, jnp.zeros((TOP, cols - NB), jnp.float32)], axis=1)
    solved = jnp.where(first_cols & holds, -own, solved)
    panel_copy.wait()
    for copy in copies:
        copy.wait()

    def place(k, carry):
        index = where_ref[k]

        @pl.when(index >= 0)
        def _():
            a_buf[pl.ds(index, 1), :] = old_top_ref[pl.ds(k, 1), :]
            p_buf[pl.ds(index, 1), :] = old_lead_ref[pl.ds(k, 1), :]

        return carry

    lax.fori_loop(0, TOP, place, 0)
    dropped = (lax.broadcasted_iota(jnp.int32, (rows, cols), 1) < NB) & holds
    outs = []
    for i in range(CHUNKS):
        part = pl.ds(rows * i, rows)
        kept = jnp.where(dropped, 0.0, a_buf[part, :])
        a_buf[part, :] = kept - dot(p_buf[part, :], solved)
        if i == 0:

            @pl.when(my_row < 2)
            def _():
                half = jnp.where(my_row == 0, upper[:NB], upper[NB:])
                corner = jnp.where(my_row == 0, lu[:NB, :], lu[NB:, :])
                corner = jnp.where(my_col == 0, corner[:, :NB], corner[:, NB:])
                corner = jnp.concatenate(
                    [corner, jnp.zeros((NB, cols - NB), jnp.float32)], axis=1
                )
                a_buf[:NB, :] = jnp.where(first_cols[:NB] & holds, corner, half)

        out = pltpu.make_async_copy(a_buf.at[part], out_ref.at[part], out_sem.at[i])
        out.start()
        outs.append(out)
    for out in outs:
        out.wait()


def finish(matrix, panel, lead, new_top, old_top, old_lead, place_index):
    any_spec = pl.BlockSpec(memory_space=pl.ANY)
    vmem = pl.BlockSpec(memory_space=pltpu.VMEM)
    return pl.pallas_call(
        finish_kernel,
        out_shape=jax.ShapeDtypeStruct(matrix.shape, jnp.float32),
        in_specs=[pl.BlockSpec(memory_space=pltpu.SMEM), any_spec, any_spec] + [vmem] * 4,
        out_specs=any_spec,
        scratch_shapes=[
            pltpu.VMEM(matrix.shape, jnp.float32),
            pltpu.VMEM(panel.shape, jnp.float32),
            pltpu.VMEM((TOP, TOP), jnp.float32),
            pltpu.VMEM((TOP, TOP), jnp.float32),
            pltpu.VMEM((TOP, TOP), jnp.float32),
            pltpu.SemaphoreType.DMA((CHUNKS,)),
            pltpu.SemaphoreType.DMA,
            pltpu.SemaphoreType.DMA((CHUNKS,)),
        ],
        name="finish",
    )(place_index, matrix, panel, lead, new_top, old_top, old_lead)


def shards(matrix, pivots):
    grid_rows = lax.axis_size("row")
    my_row = lax.axis_index("row")
    my_col = lax.axis_index("col")
    pivot = pivots.reshape(-1)
    owned = pivot // NB % grid_rows == my_row
    local = pivot // NB // grid_rows * NB + pivot % NB
    lead_cols = matrix[:, :NB]
    zero = jnp.zeros_like(lead_cols)
    mine = jnp.concatenate(
        [jnp.where(my_col == 0, lead_cols, zero), jnp.where(my_col == 1, lead_cols, zero)], axis=1
    )
    panel = lax.psum(mine, "col")

    def picked(array):
        return jnp.where(owned[:, None], array[jnp.where(owned, local, 0)], 0.0)

    def top_of(array):
        part = array[:NB]
        none = jnp.zeros_like(part)
        return jnp.concatenate(
            [jnp.where(my_row == 0, part, none), jnp.where(my_row == 1, part, none)], axis=0
        )

    new_top, lead, old_top, old_lead = lax.psum(
        (picked(matrix), picked(panel), top_of(matrix), top_of(panel)), "row"
    )
    return finish(
        matrix, panel, lead, new_top, old_top, old_lead, jnp.where(owned, local, -1)
    )


def solution(mesh):
    placed = (P("row", "col"), P())
    return jax.shard_map(
        shards, mesh=mesh, in_specs=placed, out_specs=P("row", "col"), check_vma=False
    )
```

```python
import jax
import jax.numpy as jnp
from jax import lax
from jax.experimental import pallas as pl
from jax.experimental.pallas import tpu as pltpu
from jax.sharding import PartitionSpec as P

NB = 64
TOP = 2 * NB
SUB = 8
CHUNKS = 8
HIGHEST = lax.Precision.HIGHEST
MESH = pl.DeviceIdType.MESH


def dot(a, b):
    return lax.dot_general(
        a, b, (((1,), (0,)), ((), ())), precision=HIGHEST, preferred_element_type=jnp.float32
    )


def factor(a_ref, lu_ref, linv_ref, uinv_ref):
    n = TOP // SUB
    lane = lax.broadcasted_iota(jnp.int32, (SUB, TOP), 1)
    sub = lax.broadcasted_iota(jnp.int32, (SUB, TOP), 0)
    a = [a_ref[SUB * i : SUB * (i + 1), :] for i in range(n)]
    eye = [jnp.where(lane == sub + SUB * i, 1.0, 0.0).astype(jnp.float32) for i in range(n)]
    low = list(eye)
    upp = list(eye)
    weights = jnp.ones((SUB, TOP), jnp.float32)
    for k in range(TOP):
        kb, ks = divmod(k, SUB)
        row = jnp.broadcast_to(a[kb][ks : ks + 1, :], (SUB, TOP))
        low_row = jnp.broadcast_to(low[kb][ks : ks + 1, :], (SUB, TOP))
        weight = 1.0 / jnp.broadcast_to(row[:, k : k + 1], (SUB, TOP))
        weights = jnp.where(lane == k, weight, weights)
        scaled = jnp.where(lane > k, row * weight, 0.0)
        low_scaled = low_row * weight
        for i in range(kb, n):
            column = jnp.broadcast_to(a[i][:, k : k + 1], (SUB, TOP))
            if i == kb:
                column = jnp.where(sub > ks, column, 0.0)
            a[i] = a[i] - column * scaled
            low[i] = low[i] - column * low_scaled
        for i in range(kb + 1):
            column = jnp.broadcast_to(upp[i][:, k : k + 1], (SUB, TOP))
            upp[i] = upp[i] - column * scaled
    for i in range(n):
        part = slice(SUB * i, SUB * (i + 1))
        lu_ref[part, :] = jnp.where(sub + SUB * i > lane, a[i] * weights, a[i])
        linv_ref[part, :] = low[i]
        uinv_ref[part, :] = upp[i] * weights


def finish_kernel(
    where_ref,
    a_ref,
    panel_ref,
    lead_ref,
    new_top_ref,
    old_top_ref,
    old_lead_ref,
    out_ref,
    a_buf,
    p_buf,
    lu,
    linv,
    uinv,
    in_sem,
    panel_sem,
    out_sem,
):
    my_row = lax.axis_index("row")
    my_col = lax.axis_index("col")
    rows = a_buf.shape[0] // CHUNKS
    copies = [
        pltpu.make_async_copy(
            a_ref.at[pl.ds(rows * i, rows)], a_buf.at[pl.ds(rows * i, rows)], in_sem.at[i]
        )
        for i in range(CHUNKS)
    ]
    panel_copy = pltpu.make_async_copy(panel_ref, p_buf, panel_sem)
    panel_copy.start()
    for copy in copies:
        copy.start()
    factor(lead_ref, lu, linv, uinv)
    cols = a_buf.shape[1]
    upper = dot(linv[...], new_top_ref[...])
    solved = dot(uinv[...], upper)
    holds = my_col < 2
    first_cols = lax.broadcasted_iota(jnp.int32, (TOP, cols), 1) < NB
    own = jnp.where(my_col == 0, uinv[:, :NB], uinv[:, NB:])
    own = jnp.concatenate([own, jnp.zeros((TOP, cols - NB), jnp.float32)], axis=1)
    solved = jnp.where(first_cols & holds, -own, solved)
    panel_copy.wait()
    for copy in copies:
        copy.wait()

    def place(k, carry):
        index = where_ref[k]

        @pl.when(index >= 0)
        def _():
            a_buf[pl.ds(index, 1), :] = old_top_ref[pl.ds(k, 1), :]
            p_buf[pl.ds(index, 1), :] = old_lead_ref[pl.ds(k, 1), :]

        return carry

    lax.fori_loop(0, TOP, place, 0)
    dropped = (lax.broadcasted_iota(jnp.int32, (rows, cols), 1) < NB) & holds
    outs = []
    for i in range(CHUNKS):
        part = pl.ds(rows * i, rows)
        kept = jnp.where(dropped, 0.0, a_buf[part, :])
        a_buf[part, :] = kept - dot(p_buf[part, :], solved)
        if i == 0:

            @pl.when(my_row < 2)
            def _():
                half = jnp.where(my_row == 0, upper[:NB], upper[NB:])
                corner = jnp.where(my_row == 0, lu[:NB, :], lu[NB:, :])
                corner = jnp.where(my_col == 0, corner[:, :NB], corner[:, NB:])
                corner = jnp.concatenate(
                    [corner, jnp.zeros((NB, cols - NB), jnp.float32)], axis=1
                )
                a_buf[:NB, :] = jnp.where(first_cols[:NB] & holds, corner, half)

        out = pltpu.make_async_copy(a_buf.at[part], out_ref.at[part], out_sem.at[i])
        out.start()
        outs.append(out)
    for out in outs:
        out.wait()


def finish(matrix, panel, lead, new_top, old_top, old_lead, place_index):
    any_spec = pl.BlockSpec(memory_space=pl.ANY)
    vmem = pl.BlockSpec(memory_space=pltpu.VMEM)
    return pl.pallas_call(
        finish_kernel,
        out_shape=jax.ShapeDtypeStruct(matrix.shape, jnp.float32),
        in_specs=[pl.BlockSpec(memory_space=pltpu.SMEM), any_spec, any_spec] + [vmem] * 4,
        out_specs=any_spec,
        scratch_shapes=[
            pltpu.VMEM(matrix.shape, jnp.float32),
            pltpu.VMEM(panel.shape, jnp.float32),
            pltpu.VMEM((TOP, TOP), jnp.float32),
            pltpu.VMEM((TOP, TOP), jnp.float32),
            pltpu.VMEM((TOP, TOP), jnp.float32),
            pltpu.SemaphoreType.DMA((CHUNKS,)),
            pltpu.SemaphoreType.DMA,
            pltpu.SemaphoreType.DMA((CHUNKS,)),
        ],
        name="finish",
    )(place_index, matrix, panel, lead, new_top, old_top, old_lead)


def move_kernel(
    where_ref,
    a_ref,
    panel_ref,
    new_ref,
    old_ref,
    lead_ref,
    old_lead_ref,
    a_buf,
    pack,
    picked,
    parts,
    whole,
    picked_lead,
    parts_lead,
    whole_lead,
    load_sem,
    slice_send,
    slice_recv,
    spread_send,
    pair_send,
    pair_recv,
    part_send,
    part_recv,
    top_send,
    top_recv,
    whole_send,
    whole_recv,
    lead_part_send,
    lead_part_recv,
    lead_top_send,
    lead_top_recv,
    lead_whole_send,
    lead_whole_recv,
):
    rows_dev = lax.axis_size("row")
    chips = lax.axis_size("col") // 2
    my_row = lax.axis_index("row")
    my_col = lax.axis_index("col")
    chip = my_col // 2
    core = my_col % 2
    chunk = TOP // rows_dev
    half_rows = a_buf.shape[0] // 2
    slice_rows = half_rows // chips

    load = pltpu.make_async_copy(a_ref, a_buf, load_sem)
    load.start()
    barrier = pltpu.get_barrier_semaphore()
    for j in range(1, rows_dev):
        pl.semaphore_signal(
            barrier, inc=1, device_id={"row": lax.rem(my_row + j, rows_dev)}, device_id_type=MESH
        )
    for j in range(1, chips):
        pl.semaphore_signal(
            barrier,
            inc=1,
            device_id={"col": lax.rem(chip + j, chips) * 2 + core},
            device_id_type=MESH,
        )
    pl.semaphore_signal(
        barrier, inc=1, device_id={"col": chip * 2 + 1 - core}, device_id_type=MESH
    )
    load.wait()

    def pick(table, target):
        def body(k, carry):
            index = where_ref[k]
            row = table[pl.ds(jnp.maximum(index, 0), 1), :]
            target[pl.ds(k, 1), :] = jnp.where(index >= 0, row, 0.0)
            return carry

        lax.fori_loop(0, TOP, body, 0)

    first = lax.broadcasted_iota(jnp.int32, (slice_rows, TOP), 1) < NB

    @pl.when(chip == 0)
    def _():
        for s in range(chips):
            low = a_buf[slice_rows * s : slice_rows * (s + 1), :TOP]
            high = a_buf[half_rows + slice_rows * s : half_rows + slice_rows * (s + 1), :TOP]
            at_zero = jnp.where(core == 0, low, high)
            shifted = jnp.where(core == 0, high, low)
            pack[core, s] = jnp.where(first, at_zero, pltpu.roll(shifted, NB, 1))

    pick(a_buf, picked)
    pl.semaphore_wait(barrier, rows_dev - 1 + chips)

    def slice_copy(s, t, send):
        return pltpu.make_async_remote_copy(
            src_ref=pack.at[core, s],
            dst_ref=pack.at[core, s],
            send_sem=send,
            recv_sem=slice_recv.at[s],
            device_id={"col": t * 2 + core},
            device_id_type=MESH,
        )

    @pl.when(chip == 0)
    def _():
        for s in range(1, chips):
            slice_copy(s, s, slice_send.at[s]).start()

    def part_copy(j, source, target, send, recv):
        d = lax.rem(my_row + j, rows_dev)
        return pltpu.make_async_remote_copy(
            src_ref=source.at[pl.ds(d * chunk, chunk)],
            dst_ref=target.at[my_row],
            send_sem=send.at[j],
            recv_sem=recv.at[my_row],
            device_id={"row": d},
            device_id_type=MESH,
        )

    def top_copy(d, source, target, send, recv):
        owner = d * chunk // NB
        start = d * chunk - owner * NB
        return pltpu.make_async_remote_copy(
            src_ref=source.at[pl.ds(start, chunk), :],
            dst_ref=target.at[d, pl.ds(chunk, chunk)],
            send_sem=send.at[d],
            recv_sem=recv,
            device_id={"row": d},
            device_id_type=MESH,
        )

    def whole_copy(j, target, send, recv):
        return pltpu.make_async_remote_copy(
            src_ref=target.at[my_row],
            dst_ref=target.at[my_row],
            send_sem=send.at[j],
            recv_sem=recv.at[my_row],
            device_id={"row": lax.rem(my_row + j, rows_dev)},
            device_id_type=MESH,
        )

    def start_rows(source, table, parts, whole, send, recv, t_send, t_recv):
        for j in range(1, rows_dev):
            part_copy(j, source, parts, send, recv).start()
        parts[my_row] = source[pl.ds(pl.multiple_of(my_row * chunk, chunk), chunk), :]
        for d in range(rows_dev):
            owner = d * chunk // NB
            if d == owner:

                @pl.when(my_row == owner)
                def _():
                    start = d * chunk - owner * NB
                    whole[d, chunk:] = table[start : start + chunk, :]

            else:

                @pl.when(my_row == owner)
                def _():
                    top_copy(d, table, whole, t_send, t_recv).start()

    def join_rows(source, table, parts, whole, send, recv, t_send, t_recv, w_send, w_recv):
        for j in range(1, rows_dev):
            s = lax.rem(my_row + j, rows_dev)
            pltpu.make_async_remote_copy(
                src_ref=source.at[pl.ds(0, chunk)],
                dst_ref=parts.at[s],
                send_sem=send.at[j],
                recv_sem=recv.at[s],
                device_id={"row": s},
                device_id_type=MESH,
            ).wait_recv()
        total = parts[0]
        for s in range(1, rows_dev):
            total = total + parts[s]
        whole[my_row, :chunk] = total
        for d in range(rows_dev):
            if d != d * chunk // NB:

                @pl.when(my_row == d)
                def _():
                    top_copy(d, table, whole, t_send, t_recv).wait_recv()

        for j in range(1, rows_dev):
            whole_copy(j, whole, w_send, w_recv).start()

    def end_rows(source, table, parts, whole, new, old, send, recv, t_send, t_recv, w_send, w_recv):
        for j in range(1, rows_dev):
            s = lax.rem(my_row + j, rows_dev)
            pltpu.make_async_remote_copy(
                src_ref=whole.at[s],
                dst_ref=whole.at[s],
                send_sem=w_send.at[j],
                recv_sem=w_recv.at[s],
                device_id={"row": s},
                device_id_type=MESH,
            ).wait_recv()
        for d in range(rows_dev):
            new[chunk * d : chunk * (d + 1), :] = whole[d, :chunk]
            old[chunk * d : chunk * (d + 1), :] = whole[d, chunk:]
        for j in range(1, rows_dev):
            part_copy(j, source, parts, send, recv).wait_send()
            whole_copy(j, whole, w_send, w_recv).wait_send()
        for d in range(rows_dev):
            owner = d * chunk // NB
            if d != owner:

                @pl.when(my_row == owner)
                def _():
                    top_copy(d, table, whole, t_send, t_recv).wait_send()

    main = (part_send, part_recv, top_send, top_recv)
    start_rows(picked, a_buf, parts, whole, *main)

    @pl.when(chip != 0)
    def _():
        slice_copy(chip, chip, slice_send.at[0]).wait_recv()

    for j in range(1, chips):
        t = lax.rem(chip + j, chips)

        @pl.when(t != 0)
        def _():
            slice_copy(chip, t, spread_send.at[j]).start()

    join_rows(picked, a_buf, parts, whole, *main, whole_send, whole_recv)

    groups = min(4, chips)
    per = chips // groups

    def pair_copy(g, which):
        return pltpu.make_async_remote_copy(
            src_ref=pack.at[which, pl.ds(g * per, per)],
            dst_ref=pack.at[which, pl.ds(g * per, per)],
            send_sem=pair_send.at[g],
            recv_sem=pair_recv.at[g],
            device_id={"col": chip * 2 + 1 - core},
            device_id_type=MESH,
        )

    for g in range(groups):

        @pl.when(chip != 0)
        def _():
            for s in range(g * per, (g + 1) * per):

                @pl.when(chip != s)
                def _():
                    slice_copy(s, chip, slice_send.at[0]).wait_recv()

        pair_copy(g, core).start()

    for g in range(groups):
        pair_copy(g, 1 - core).wait_recv()
        for s in range(g * per, (g + 1) * per):
            zero_pack = pack[0, s]
            one_pack = pack[1, s]
            low = slice(slice_rows * s, slice_rows * (s + 1))
            high = slice(half_rows + slice_rows * s, half_rows + slice_rows * (s + 1))
            panel_ref[low, :] = jnp.where(first, zero_pack, one_pack)
            panel_ref[high, :] = pltpu.roll(jnp.where(first, one_pack, zero_pack), NB, 1)

    pick(panel_ref, picked_lead)
    small = (lead_part_send, lead_part_recv, lead_top_send, lead_top_recv)
    start_rows(picked_lead, panel_ref, parts_lead, whole_lead, *small)
    join_rows(
        picked_lead, panel_ref, parts_lead, whole_lead, *small, lead_whole_send, lead_whole_recv
    )
    end_rows(picked, a_buf, parts, whole, new_ref, old_ref, *main, whole_send, whole_recv)
    end_rows(
        picked_lead,
        panel_ref,
        parts_lead,
        whole_lead,
        lead_ref,
        old_lead_ref,
        *small,
        lead_whole_send,
        lead_whole_recv,
    )

    @pl.when(chip == 0)
    def _():
        for s in range(1, chips):
            slice_copy(s, s, slice_send.at[s]).wait_send()

    for j in range(1, chips):
        t = lax.rem(chip + j, chips)

        @pl.when(t != 0)
        def _():
            slice_copy(chip, t, spread_send.at[j]).wait_send()

    for g in range(groups):
        pair_copy(g, core).wait_send()


def move(matrix, place_index):
    rows_dev = lax.axis_size("row")
    chips = lax.axis_size("col") // 2
    chunk = TOP // rows_dev
    rows, cols = matrix.shape
    dma = pltpu.SemaphoreType.DMA
    f32 = jnp.float32
    vmem = pl.BlockSpec(memory_space=pltpu.VMEM)

    def row_sems():
        return [
            dma((rows_dev,)),
            dma((rows_dev,)),
            dma((rows_dev,)),
            dma,
        ]

    return pl.pallas_call(
        move_kernel,
        out_shape=[
            jax.ShapeDtypeStruct((rows, TOP), f32),
            jax.ShapeDtypeStruct((TOP, cols), f32),
            jax.ShapeDtypeStruct((TOP, cols), f32),
            jax.ShapeDtypeStruct((TOP, TOP), f32),
            jax.ShapeDtypeStruct((TOP, TOP), f32),
        ],
        in_specs=[
            pl.BlockSpec(memory_space=pltpu.SMEM),
            pl.BlockSpec(memory_space=pl.ANY),
        ],
        out_specs=[vmem] * 5,
        scratch_shapes=[
            pltpu.VMEM((rows, cols), f32),
            pltpu.VMEM((2, chips, rows // 2 // chips, TOP), f32),
            pltpu.VMEM((TOP, cols), f32),
            pltpu.VMEM((rows_dev, chunk, cols), f32),
            pltpu.VMEM((rows_dev, 2 * chunk, cols), f32),
            pltpu.VMEM((TOP, TOP), f32),
            pltpu.VMEM((rows_dev, chunk, TOP), f32),
            pltpu.VMEM((rows_dev, 2 * chunk, TOP), f32),
            dma,
            dma((chips,)),
            dma((chips,)),
            dma((chips,)),
            dma((4,)),
            dma((4,)),
            *row_sems(),
            dma((rows_dev,)),
            dma((rows_dev,)),
            *row_sems(),
            dma((rows_dev,)),
            dma((rows_dev,)),
        ],
        compiler_params=pltpu.CompilerParams(collective_id=0, has_side_effects=True),
        name="move",
    )(place_index, matrix)


def shards(matrix, pivots):
    my_row = lax.axis_index("row")
    grid_rows = lax.axis_size("row")
    pivot = pivots.reshape(-1)
    owned = pivot // NB % grid_rows == my_row
    local = pivot // NB // grid_rows * NB + pivot % NB
    place_index = jnp.where(owned, local, -1)
    panel, new_top, old_top, lead, old_lead = move(matrix, place_index)
    return finish(matrix, panel, lead, new_top, old_top, old_lead, place_index)

def solution(mesh):
    placed = (P("row", "col"), P())
    return jax.shard_map(
        shards, mesh=mesh, in_specs=placed, out_specs=P("row", "col"), check_vma=False
    )
```

```python
import jax
import jax.numpy as jnp
from jax import lax
from jax.experimental import pallas as pl
from jax.experimental.pallas import tpu as pltpu
from jax.sharding import PartitionSpec as P

NB = 64
TOP = 2 * NB
SUB = 8
CHUNKS = 8
PLACES = 8
HIGHEST = lax.Precision.HIGHEST
MESH = pl.DeviceIdType.MESH


def dot(a, b):
    return lax.dot_general(
        a, b, (((1,), (0,)), ((), ())), precision=HIGHEST, preferred_element_type=jnp.float32
    )


def halves(x):
    high = x.astype(jnp.bfloat16)
    return high, (x - high.astype(jnp.float32)).astype(jnp.bfloat16)


def dot_pair(a, b):
    return lax.dot_general(
        a, b, (((1,), (0,)), ((), ())), preferred_element_type=jnp.float32
    )


def spread(block, lane):
    return jnp.broadcast_to(block[:, lane : lane + 1], block.shape)


def line(block, row):
    return jnp.broadcast_to(block[row : row + 1, :], block.shape)


def factor(a_ref, lu_ref, linv_ref, uinv_ref):
    n = TOP // SUB
    lane = lax.broadcasted_iota(jnp.int32, (SUB, TOP), 1)
    sub = lax.broadcasted_iota(jnp.int32, (SUB, TOP), 0)
    a = [a_ref[SUB * i : SUB * (i + 1), :] for i in range(n)]
    low = [jnp.where(lane == sub + SUB * i, 1.0, 0.0).astype(jnp.float32) for i in range(n)]
    upp = list(low)
    weights = jnp.ones((SUB, TOP), jnp.float32)
    for b in range(n):
        first = SUB * b
        cols = [spread(a[b], first + j) for j in range(SUB)]
        weight, entry, a_line, low_line = [], [], [], []
        for k in range(SUB):
            weight.append(1.0 / line(cols[k], k))
            weights = jnp.where(lane == first + k, weight[k], weights)
            entry.append([line(cols[j], k) if j > k else None for j in range(SUB)])
            a_line.append(jnp.where(lane > first + k, line(a[b], k), 0.0))
            low_line.append(line(low[b], k))
            if k < SUB - 1:
                multiplier = jnp.where(sub > k, cols[k] * weight[k], 0.0)
                for j in range(k + 1, SUB):
                    cols[j] = cols[j] - multiplier * entry[k][j]
                a[b] = a[b] - multiplier * a_line[k]
                low[b] = low[b] - multiplier * low_line[k]

        def multipliers(cols):
            cols = list(cols)
            for k in range(SUB):
                cols[k] = cols[k] * weight[k]
                for j in range(k + 1, SUB):
                    cols[j] = cols[j] - cols[k] * entry[k][j]
            return cols

        for i in range(b + 1, n):
            part = multipliers([spread(a[i], first + j) for j in range(SUB)])
            for k in range(SUB):
                a[i] = a[i] - part[k] * a_line[k]
                low[i] = low[i] - part[k] * low_line[k]
        for i in range(b + 1):
            if i == b:
                part = [jnp.where(sub == j, 1.0, 0.0).astype(jnp.float32) for j in range(SUB)]
            else:
                part = [spread(upp[i], first + j) for j in range(SUB)]
            part = multipliers(part)
            for k in range(SUB):
                upp[i] = upp[i] - part[k] * a_line[k]
    for i in range(n):
        part = slice(SUB * i, SUB * (i + 1))
        lu_ref[part, :] = jnp.where(sub + SUB * i > lane, a[i] * weights, a[i])
        linv_ref[part, :] = low[i]
        uinv_ref[part, :] = upp[i] * weights


def finish_kernel(
    where_ref,
    a_ref,
    panel_ref,
    lead_ref,
    new_top_ref,
    old_top_ref,
    old_lead_ref,
    out_ref,
    a_buf,
    p_buf,
    lu,
    linv,
    uinv,
    in_sem,
    panel_sem,
    out_sem,
):
    my_row = lax.axis_index("row")
    my_col = lax.axis_index("col")
    rows = a_buf.shape[0] // CHUNKS
    copies = [
        pltpu.make_async_copy(
            a_ref.at[pl.ds(rows * i, rows)], a_buf.at[pl.ds(rows * i, rows)], in_sem.at[i]
        )
        for i in range(CHUNKS)
    ]
    panel_copy = pltpu.make_async_copy(panel_ref, p_buf, panel_sem)
    panel_copy.start()
    for copy in copies:
        copy.start()
    factor(lead_ref, lu, linv, uinv)
    cols = a_buf.shape[1]
    upper = dot(linv[...], new_top_ref[...])
    solved = dot(uinv[...], upper)
    holds = my_col < 2
    first_cols = lax.broadcasted_iota(jnp.int32, (TOP, cols), 1) < NB
    own = jnp.where(my_col == 0, uinv[:, :NB], uinv[:, NB:])
    own = jnp.concatenate([own, jnp.zeros((TOP, cols - NB), jnp.float32)], axis=1)
    solved = jnp.where(first_cols & holds, -own, solved)
    high, rest = halves(solved)
    twice = jnp.concatenate([high, high], axis=0)
    panel_copy.wait()
    for copy in copies:
        copy.wait()

    def place(step, carry):
        for j in range(PLACES):
            k = step * PLACES + j
            index = where_ref[k]

            @pl.when(index >= 0)
            def _():
                a_buf[pl.ds(index, 1), :] = old_top_ref[pl.ds(k, 1), :]
                p_buf[pl.ds(index, 1), :] = old_lead_ref[pl.ds(k, 1), :]

        return carry

    lax.fori_loop(0, TOP // PLACES, place, 0)
    dropped = (lax.broadcasted_iota(jnp.int32, (rows, cols), 1) < NB) & holds
    outs = []
    for i in range(CHUNKS):
        part = pl.ds(rows * i, rows)
        kept = jnp.where(dropped, 0.0, a_buf[part, :])
        left, left_rest = halves(p_buf[part, :])
        product = dot_pair(jnp.concatenate([left, left_rest], axis=1), twice)
        a_buf[part, :] = kept - (product + dot_pair(left, rest))
        if i == 0:

            @pl.when(my_row < 2)
            def _():
                half = jnp.where(my_row == 0, upper[:NB], upper[NB:])
                corner = jnp.where(my_row == 0, lu[:NB, :], lu[NB:, :])
                corner = jnp.where(my_col == 0, corner[:, :NB], corner[:, NB:])
                corner = jnp.concatenate(
                    [corner, jnp.zeros((NB, cols - NB), jnp.float32)], axis=1
                )
                a_buf[:NB, :] = jnp.where(first_cols[:NB] & holds, corner, half)

        out = pltpu.make_async_copy(a_buf.at[part], out_ref.at[part], out_sem.at[i])
        out.start()
        outs.append(out)
    for out in outs:
        out.wait()


def finish(matrix, panel, lead, new_top, old_top, old_lead, place_index):
    any_spec = pl.BlockSpec(memory_space=pl.ANY)
    vmem = pl.BlockSpec(memory_space=pltpu.VMEM)
    return pl.pallas_call(
        finish_kernel,
        out_shape=jax.ShapeDtypeStruct(matrix.shape, jnp.float32),
        in_specs=[pl.BlockSpec(memory_space=pltpu.SMEM), any_spec, any_spec] + [vmem] * 4,
        out_specs=any_spec,
        scratch_shapes=[
            pltpu.VMEM(matrix.shape, jnp.float32),
            pltpu.VMEM(panel.shape, jnp.float32),
            pltpu.VMEM((TOP, TOP), jnp.float32),
            pltpu.VMEM((TOP, TOP), jnp.float32),
            pltpu.VMEM((TOP, TOP), jnp.float32),
            pltpu.SemaphoreType.DMA((CHUNKS,)),
            pltpu.SemaphoreType.DMA,
            pltpu.SemaphoreType.DMA((CHUNKS,)),
        ],
        name="finish",
    )(place_index, matrix, panel, lead, new_top, old_top, old_lead)


def move_kernel(
    where_ref,
    a_ref,
    panel_ref,
    new_ref,
    old_ref,
    lead_ref,
    old_lead_ref,
    a_buf,
    pack,
    picked,
    parts,
    whole,
    picked_lead,
    parts_lead,
    whole_lead,
    load_sem,
    slice_send,
    slice_recv,
    spread_send,
    pair_send,
    pair_recv,
    part_send,
    part_recv,
    top_send,
    top_recv,
    whole_send,
    whole_recv,
    lead_part_send,
    lead_part_recv,
    lead_top_send,
    lead_top_recv,
    lead_whole_send,
    lead_whole_recv,
):
    rows_dev = lax.axis_size("row")
    chips = lax.axis_size("col") // 2
    my_row = lax.axis_index("row")
    my_col = lax.axis_index("col")
    chip = my_col // 2
    core = my_col % 2
    chunk = TOP // rows_dev
    half_rows = a_buf.shape[0] // 2
    slice_rows = half_rows // chips

    load = pltpu.make_async_copy(a_ref, a_buf, load_sem)
    load.start()
    barrier = pltpu.get_barrier_semaphore()
    for j in range(1, rows_dev):
        pl.semaphore_signal(
            barrier, inc=1, device_id={"row": lax.rem(my_row + j, rows_dev)}, device_id_type=MESH
        )
    for j in range(1, chips):
        pl.semaphore_signal(
            barrier,
            inc=1,
            device_id={"col": lax.rem(chip + j, chips) * 2 + core},
            device_id_type=MESH,
        )
    pl.semaphore_signal(
        barrier, inc=1, device_id={"col": chip * 2 + 1 - core}, device_id_type=MESH
    )
    load.wait()

    def pick(table, target):
        def body(k, carry):
            index = where_ref[k]
            row = table[pl.ds(jnp.maximum(index, 0), 1), :]
            target[pl.ds(k, 1), :] = jnp.where(index >= 0, row, 0.0)
            return carry

        lax.fori_loop(0, TOP, body, 0)

    first = lax.broadcasted_iota(jnp.int32, (slice_rows, TOP), 1) < NB

    @pl.when(chip == 0)
    def _():
        for s in range(chips):
            low = a_buf[slice_rows * s : slice_rows * (s + 1), :TOP]
            high = a_buf[half_rows + slice_rows * s : half_rows + slice_rows * (s + 1), :TOP]
            at_zero = jnp.where(core == 0, low, high)
            shifted = jnp.where(core == 0, high, low)
            pack[core, s] = jnp.where(first, at_zero, pltpu.roll(shifted, NB, 1))

    pick(a_buf, picked)
    pl.semaphore_wait(barrier, rows_dev - 1 + chips)

    def slice_copy(s, t, send):
        return pltpu.make_async_remote_copy(
            src_ref=pack.at[core, s],
            dst_ref=pack.at[core, s],
            send_sem=send,
            recv_sem=slice_recv.at[s],
            device_id={"col": t * 2 + core},
            device_id_type=MESH,
        )

    @pl.when(chip == 0)
    def _():
        for s in range(1, chips):
            slice_copy(s, s, slice_send.at[s]).start()

    def part_copy(j, source, target, send, recv):
        d = lax.rem(my_row + j, rows_dev)
        return pltpu.make_async_remote_copy(
            src_ref=source.at[pl.ds(d * chunk, chunk)],
            dst_ref=target.at[my_row],
            send_sem=send.at[j],
            recv_sem=recv.at[my_row],
            device_id={"row": d},
            device_id_type=MESH,
        )

    def top_copy(d, source, target, send, recv):
        owner = d * chunk // NB
        start = d * chunk - owner * NB
        return pltpu.make_async_remote_copy(
            src_ref=source.at[pl.ds(start, chunk), :],
            dst_ref=target.at[d, pl.ds(chunk, chunk)],
            send_sem=send.at[d],
            recv_sem=recv,
            device_id={"row": d},
            device_id_type=MESH,
        )

    def whole_copy(j, target, send, recv):
        return pltpu.make_async_remote_copy(
            src_ref=target.at[my_row],
            dst_ref=target.at[my_row],
            send_sem=send.at[j],
            recv_sem=recv.at[my_row],
            device_id={"row": lax.rem(my_row + j, rows_dev)},
            device_id_type=MESH,
        )

    def start_rows(source, table, parts, whole, send, recv, t_send, t_recv):
        for j in range(1, rows_dev):
            part_copy(j, source, parts, send, recv).start()
        parts[my_row] = source[pl.ds(pl.multiple_of(my_row * chunk, chunk), chunk), :]
        for d in range(rows_dev):
            owner = d * chunk // NB
            if d == owner:

                @pl.when(my_row == owner)
                def _():
                    start = d * chunk - owner * NB
                    whole[d, chunk:] = table[start : start + chunk, :]

            else:

                @pl.when(my_row == owner)
                def _():
                    top_copy(d, table, whole, t_send, t_recv).start()

    def join_rows(source, table, parts, whole, send, recv, t_send, t_recv, w_send, w_recv):
        for j in range(1, rows_dev):
            s = lax.rem(my_row + j, rows_dev)
            pltpu.make_async_remote_copy(
                src_ref=source.at[pl.ds(0, chunk)],
                dst_ref=parts.at[s],
                send_sem=send.at[j],
                recv_sem=recv.at[s],
                device_id={"row": s},
                device_id_type=MESH,
            ).wait_recv()
        total = parts[0]
        for s in range(1, rows_dev):
            total = total + parts[s]
        whole[my_row, :chunk] = total
        for d in range(rows_dev):
            if d != d * chunk // NB:

                @pl.when(my_row == d)
                def _():
                    top_copy(d, table, whole, t_send, t_recv).wait_recv()

        for j in range(1, rows_dev):
            whole_copy(j, whole, w_send, w_recv).start()

    def end_rows(source, table, parts, whole, new, old, send, recv, t_send, t_recv, w_send, w_recv):
        for j in range(1, rows_dev):
            s = lax.rem(my_row + j, rows_dev)
            pltpu.make_async_remote_copy(
                src_ref=whole.at[s],
                dst_ref=whole.at[s],
                send_sem=w_send.at[j],
                recv_sem=w_recv.at[s],
                device_id={"row": s},
                device_id_type=MESH,
            ).wait_recv()
        for d in range(rows_dev):
            new[chunk * d : chunk * (d + 1), :] = whole[d, :chunk]
            old[chunk * d : chunk * (d + 1), :] = whole[d, chunk:]
        for j in range(1, rows_dev):
            part_copy(j, source, parts, send, recv).wait_send()
            whole_copy(j, whole, w_send, w_recv).wait_send()
        for d in range(rows_dev):
            owner = d * chunk // NB
            if d != owner:

                @pl.when(my_row == owner)
                def _():
                    top_copy(d, table, whole, t_send, t_recv).wait_send()

    main = (part_send, part_recv, top_send, top_recv)
    start_rows(picked, a_buf, parts, whole, *main)

    @pl.when(chip != 0)
    def _():
        slice_copy(chip, chip, slice_send.at[0]).wait_recv()

    for j in range(1, chips):
        t = lax.rem(chip + j, chips)

        @pl.when(t != 0)
        def _():
            slice_copy(chip, t, spread_send.at[j]).start()

    join_rows(picked, a_buf, parts, whole, *main, whole_send, whole_recv)

    groups = min(4, chips)
    per = chips // groups

    def pair_copy(g, which):
        return pltpu.make_async_remote_copy(
            src_ref=pack.at[which, pl.ds(g * per, per)],
            dst_ref=pack.at[which, pl.ds(g * per, per)],
            send_sem=pair_send.at[g],
            recv_sem=pair_recv.at[g],
            device_id={"col": chip * 2 + 1 - core},
            device_id_type=MESH,
        )

    for g in range(groups):

        @pl.when(chip != 0)
        def _():
            for s in range(g * per, (g + 1) * per):

                @pl.when(chip != s)
                def _():
                    slice_copy(s, chip, slice_send.at[0]).wait_recv()

        pair_copy(g, core).start()

    for g in range(groups):
        pair_copy(g, 1 - core).wait_recv()
        for s in range(g * per, (g + 1) * per):
            zero_pack = pack[0, s]
            one_pack = pack[1, s]
            low = slice(slice_rows * s, slice_rows * (s + 1))
            high = slice(half_rows + slice_rows * s, half_rows + slice_rows * (s + 1))
            panel_ref[low, :] = jnp.where(first, zero_pack, one_pack)
            panel_ref[high, :] = pltpu.roll(jnp.where(first, one_pack, zero_pack), NB, 1)

    pick(panel_ref, picked_lead)
    small = (lead_part_send, lead_part_recv, lead_top_send, lead_top_recv)
    start_rows(picked_lead, panel_ref, parts_lead, whole_lead, *small)
    join_rows(
        picked_lead, panel_ref, parts_lead, whole_lead, *small, lead_whole_send, lead_whole_recv
    )
    end_rows(picked, a_buf, parts, whole, new_ref, old_ref, *main, whole_send, whole_recv)
    end_rows(
        picked_lead,
        panel_ref,
        parts_lead,
        whole_lead,
        lead_ref,
        old_lead_ref,
        *small,
        lead_whole_send,
        lead_whole_recv,
    )

    @pl.when(chip == 0)
    def _():
        for s in range(1, chips):
            slice_copy(s, s, slice_send.at[s]).wait_send()

    for j in range(1, chips):
        t = lax.rem(chip + j, chips)

        @pl.when(t != 0)
        def _():
            slice_copy(chip, t, spread_send.at[j]).wait_send()

    for g in range(groups):
        pair_copy(g, core).wait_send()


def move(matrix, place_index):
    rows_dev = lax.axis_size("row")
    chips = lax.axis_size("col") // 2
    chunk = TOP // rows_dev
    rows, cols = matrix.shape
    dma = pltpu.SemaphoreType.DMA
    f32 = jnp.float32
    vmem = pl.BlockSpec(memory_space=pltpu.VMEM)

    def row_sems():
        return [
            dma((rows_dev,)),
            dma((rows_dev,)),
            dma((rows_dev,)),
            dma,
        ]

    return pl.pallas_call(
        move_kernel,
        out_shape=[
            jax.ShapeDtypeStruct((rows, TOP), f32),
            jax.ShapeDtypeStruct((TOP, cols), f32),
            jax.ShapeDtypeStruct((TOP, cols), f32),
            jax.ShapeDtypeStruct((TOP, TOP), f32),
            jax.ShapeDtypeStruct((TOP, TOP), f32),
        ],
        in_specs=[
            pl.BlockSpec(memory_space=pltpu.SMEM),
            pl.BlockSpec(memory_space=pl.ANY),
        ],
        out_specs=[vmem] * 5,
        scratch_shapes=[
            pltpu.VMEM((rows, cols), f32),
            pltpu.VMEM((2, chips, rows // 2 // chips, TOP), f32),
            pltpu.VMEM((TOP, cols), f32),
            pltpu.VMEM((rows_dev, chunk, cols), f32),
            pltpu.VMEM((rows_dev, 2 * chunk, cols), f32),
            pltpu.VMEM((TOP, TOP), f32),
            pltpu.VMEM((rows_dev, chunk, TOP), f32),
            pltpu.VMEM((rows_dev, 2 * chunk, TOP), f32),
            dma,
            dma((chips,)),
            dma((chips,)),
            dma((chips,)),
            dma((4,)),
            dma((4,)),
            *row_sems(),
            dma((rows_dev,)),
            dma((rows_dev,)),
            *row_sems(),
            dma((rows_dev,)),
            dma((rows_dev,)),
        ],
        compiler_params=pltpu.CompilerParams(collective_id=0, has_side_effects=True),
        name="move",
    )(place_index, matrix)


def shards(matrix, pivots):
    my_row = lax.axis_index("row")
    grid_rows = lax.axis_size("row")
    pivot = pivots.reshape(-1)
    owned = pivot // NB % grid_rows == my_row
    local = pivot // NB // grid_rows * NB + pivot % NB
    place_index = jnp.where(owned, local, -1)
    panel, new_top, old_top, lead, old_lead = move(matrix, place_index)
    return finish(matrix, panel, lead, new_top, old_top, old_lead, place_index)

def solution(mesh):
    placed = (P("row", "col"), P())
    return jax.shard_map(
        shards, mesh=mesh, in_specs=placed, out_specs=P("row", "col"), check_vma=False
    )
```

```python
import jax
import jax.numpy as jnp
from jax import lax
from jax.experimental import pallas as pl
from jax.experimental.pallas import tpu as pltpu
from jax.sharding import PartitionSpec as P

NB = 64
TOP = 2 * NB
SUB = 8
CHUNKS = 8
PLACES = 8
HIGHEST = lax.Precision.HIGHEST
MESH = pl.DeviceIdType.MESH


def dot(a, b):
    return lax.dot_general(
        a, b, (((1,), (0,)), ((), ())), precision=HIGHEST, preferred_element_type=jnp.float32
    )


def place_of(pivot_ref, k):
    pivot = pivot_ref[k // NB, k % NB]
    block = pivot // NB
    grid_rows = lax.axis_size("row")
    local = block // grid_rows * NB + pivot % NB
    return jnp.where(block % grid_rows == lax.axis_index("row"), local, -1)


def halves(x):
    high = x.astype(jnp.bfloat16)
    return high, (x - high.astype(jnp.float32)).astype(jnp.bfloat16)


def dot_pair(a, b):
    return lax.dot_general(
        a, b, (((1,), (0,)), ((), ())), preferred_element_type=jnp.float32
    )


def spread(block, lane):
    return jnp.broadcast_to(block[:, lane : lane + 1], block.shape)


def line(block, row):
    return jnp.broadcast_to(block[row : row + 1, :], block.shape)


def factor(a_ref, lu_ref, linv_ref, uinv_ref):
    n = TOP // SUB
    lane = lax.broadcasted_iota(jnp.int32, (SUB, TOP), 1)
    sub = lax.broadcasted_iota(jnp.int32, (SUB, TOP), 0)
    a = [a_ref[SUB * i : SUB * (i + 1), :] for i in range(n)]
    low = [jnp.where(lane == sub + SUB * i, 1.0, 0.0).astype(jnp.float32) for i in range(n)]
    upp = list(low)
    weights = jnp.ones((SUB, TOP), jnp.float32)
    for b in range(n):
        first = SUB * b
        cols = [spread(a[b], first + j) for j in range(SUB)]
        weight, entry, a_line, low_line = [], [], [], []
        for k in range(SUB):
            weight.append(1.0 / line(cols[k], k))
            weights = jnp.where(lane == first + k, weight[k], weights)
            entry.append([line(cols[j], k) if j > k else None for j in range(SUB)])
            a_line.append(jnp.where(lane > first + k, line(a[b], k), 0.0))
            low_line.append(line(low[b], k))
            if k < SUB - 1:
                multiplier = jnp.where(sub > k, cols[k] * weight[k], 0.0)
                for j in range(k + 1, SUB):
                    cols[j] = cols[j] - multiplier * entry[k][j]
                a[b] = a[b] - multiplier * a_line[k]
                low[b] = low[b] - multiplier * low_line[k]

        def multipliers(cols):
            cols = list(cols)
            for k in range(SUB):
                cols[k] = cols[k] * weight[k]
                for j in range(k + 1, SUB):
                    cols[j] = cols[j] - cols[k] * entry[k][j]
            return cols

        for i in range(b + 1, n):
            part = multipliers([spread(a[i], first + j) for j in range(SUB)])
            for k in range(SUB):
                a[i] = a[i] - part[k] * a_line[k]
                low[i] = low[i] - part[k] * low_line[k]
        for i in range(b + 1):
            if i == b:
                part = [jnp.where(sub == j, 1.0, 0.0).astype(jnp.float32) for j in range(SUB)]
            else:
                part = [spread(upp[i], first + j) for j in range(SUB)]
            part = multipliers(part)
            for k in range(SUB):
                upp[i] = upp[i] - part[k] * a_line[k]
    for i in range(n):
        part = slice(SUB * i, SUB * (i + 1))
        lu_ref[part, :] = jnp.where(sub + SUB * i > lane, a[i] * weights, a[i])
        linv_ref[part, :] = low[i]
        uinv_ref[part, :] = upp[i] * weights


def finish_kernel(
    pivot_ref,
    a_ref,
    panel_ref,
    lead_ref,
    new_top_ref,
    old_top_ref,
    old_lead_ref,
    out_ref,
    a_buf,
    p_buf,
    lu,
    linv,
    uinv,
    in_sem,
    panel_sem,
    out_sem,
):
    my_row = lax.axis_index("row")
    my_col = lax.axis_index("col")
    rows = a_buf.shape[0] // CHUNKS
    copies = [
        pltpu.make_async_copy(
            a_ref.at[pl.ds(rows * i, rows)], a_buf.at[pl.ds(rows * i, rows)], in_sem.at[i]
        )
        for i in range(CHUNKS)
    ]
    panel_copy = pltpu.make_async_copy(panel_ref, p_buf, panel_sem)
    panel_copy.start()
    for copy in copies:
        copy.start()
    factor(lead_ref, lu, linv, uinv)
    cols = a_buf.shape[1]
    upper = dot(linv[...], new_top_ref[...])
    solved = dot(uinv[...], upper)
    holds = my_col < 2
    first_cols = lax.broadcasted_iota(jnp.int32, (TOP, cols), 1) < NB
    own = jnp.where(my_col == 0, uinv[:, :NB], uinv[:, NB:])
    own = jnp.concatenate([own, jnp.zeros((TOP, cols - NB), jnp.float32)], axis=1)
    solved = jnp.where(first_cols & holds, -own, solved)
    high, rest = halves(solved)
    twice = jnp.concatenate([high, high], axis=0)
    panel_copy.wait()
    for copy in copies:
        copy.wait()

    def place(step, carry):
        for j in range(PLACES):
            k = step * PLACES + j
            index = place_of(pivot_ref, k)

            @pl.when(index >= 0)
            def _():
                a_buf[pl.ds(index, 1), :] = old_top_ref[pl.ds(k, 1), :]
                p_buf[pl.ds(index, 1), :] = old_lead_ref[pl.ds(k, 1), :]

        return carry

    lax.fori_loop(0, TOP // PLACES, place, 0)
    dropped = (lax.broadcasted_iota(jnp.int32, (rows, cols), 1) < NB) & holds
    outs = []
    for i in range(CHUNKS):
        part = pl.ds(rows * i, rows)
        kept = jnp.where(dropped, 0.0, a_buf[part, :])
        left, left_rest = halves(p_buf[part, :])
        product = dot_pair(jnp.concatenate([left, left_rest], axis=1), twice)
        a_buf[part, :] = kept - (product + dot_pair(left, rest))
        if i == 0:

            @pl.when(my_row < 2)
            def _():
                half = jnp.where(my_row == 0, upper[:NB], upper[NB:])
                corner = jnp.where(my_row == 0, lu[:NB, :], lu[NB:, :])
                corner = jnp.where(my_col == 0, corner[:, :NB], corner[:, NB:])
                corner = jnp.concatenate(
                    [corner, jnp.zeros((NB, cols - NB), jnp.float32)], axis=1
                )
                a_buf[:NB, :] = jnp.where(first_cols[:NB] & holds, corner, half)

        out = pltpu.make_async_copy(a_buf.at[part], out_ref.at[part], out_sem.at[i])
        out.start()
        outs.append(out)
    for out in outs:
        out.wait()


def finish(matrix, panel, lead, new_top, old_top, old_lead, pivots):
    any_spec = pl.BlockSpec(memory_space=pl.ANY)
    vmem = pl.BlockSpec(memory_space=pltpu.VMEM)
    return pl.pallas_call(
        finish_kernel,
        out_shape=jax.ShapeDtypeStruct(matrix.shape, jnp.float32),
        in_specs=[pl.BlockSpec(memory_space=pltpu.SMEM), any_spec, any_spec] + [vmem] * 4,
        out_specs=any_spec,
        scratch_shapes=[
            pltpu.VMEM(matrix.shape, jnp.float32),
            pltpu.VMEM(panel.shape, jnp.float32),
            pltpu.VMEM((TOP, TOP), jnp.float32),
            pltpu.VMEM((TOP, TOP), jnp.float32),
            pltpu.VMEM((TOP, TOP), jnp.float32),
            pltpu.SemaphoreType.DMA((CHUNKS,)),
            pltpu.SemaphoreType.DMA,
            pltpu.SemaphoreType.DMA((CHUNKS,)),
        ],
        name="finish",
    )(pivots, matrix, panel, lead, new_top, old_top, old_lead)


def move_kernel(
    pivot_ref,
    a_ref,
    panel_ref,
    new_ref,
    old_ref,
    lead_ref,
    old_lead_ref,
    a_buf,
    pack,
    picked,
    parts,
    news,
    olds,
    tiles,
    tile_parts,
    tile_pair,
    leads,
    load_sem,
    slice_send,
    slice_recv,
    spread_send,
    pair_send,
    pair_recv,
    part_send,
    part_recv,
    top_send,
    top_recv,
    new_send,
    new_recv,
    old_send,
    old_recv,
    tile_send,
    tile_recv,
    fan_send,
    fan_recv,
    lead_send,
    lead_recv,
):
    rows_dev = lax.axis_size("row")
    cols_dev = lax.axis_size("col")
    chips = cols_dev // 2
    my_row = lax.axis_index("row")
    my_col = lax.axis_index("col")
    chip = my_col // 2
    core = my_col % 2
    chunk = TOP // rows_dev
    half_rows = a_buf.shape[0] // 2
    slice_rows = half_rows // chips

    load = pltpu.make_async_copy(a_ref, a_buf, load_sem)
    load.start()
    barrier = pltpu.get_barrier_semaphore()
    for j in range(1, rows_dev):
        pl.semaphore_signal(
            barrier, inc=1, device_id={"row": lax.rem(my_row + j, rows_dev)}, device_id_type=MESH
        )
    for j in range(1, cols_dev):
        pl.semaphore_signal(
            barrier, inc=1, device_id={"col": lax.rem(my_col + j, cols_dev)}, device_id_type=MESH
        )
    load.wait()

    def pick(step, carry):
        for j in range(PLACES):
            k = step * PLACES + j
            index = place_of(pivot_ref, k)
            row = a_buf[pl.ds(jnp.maximum(index, 0), 1), :]
            picked[pl.ds(k, 1), :] = jnp.where(index >= 0, row, 0.0)
        return carry

    lax.fori_loop(0, TOP // PLACES, pick, 0)
    first = lax.broadcasted_iota(jnp.int32, (slice_rows, TOP), 1) < NB
    first_tile = lax.broadcasted_iota(jnp.int32, (chunk, TOP), 1) < NB

    def top_start(d):
        return d * chunk - d * chunk // NB * NB

    @pl.when(chip == 0)
    def _():
        for d in range(rows_dev):
            start = top_start(d)
            top = pltpu.roll(a_buf[start : start + chunk, :TOP], NB, 1)
            top = jnp.where(my_row == d * chunk // NB, top, 0.0)
            tiles[d] = jnp.where(first_tile, picked[chunk * d : chunk * (d + 1), :TOP], top)
        for s in range(chips):
            low = a_buf[slice_rows * s : slice_rows * (s + 1), :TOP]
            high = a_buf[half_rows + slice_rows * s : half_rows + slice_rows * (s + 1), :TOP]
            at_zero = jnp.where(core == 0, low, high)
            shifted = jnp.where(core == 0, high, low)
            pack[core, s] = jnp.where(first, at_zero, pltpu.roll(shifted, NB, 1))

    pl.semaphore_wait(barrier, rows_dev + cols_dev - 2)

    def to_row(source, target, send, recv, d):
        return pltpu.make_async_remote_copy(
            src_ref=source,
            dst_ref=target,
            send_sem=send,
            recv_sem=recv,
            device_id={"row": d},
            device_id_type=MESH,
        )

    def to_col(source, target, send, recv, q):
        return pltpu.make_async_remote_copy(
            src_ref=source,
            dst_ref=target,
            send_sem=send,
            recv_sem=recv,
            device_id={"col": q},
            device_id_type=MESH,
        )

    def other(j):
        return lax.rem(my_row + j, rows_dev)

    def tile_copy(j):
        d = other(j)
        return to_row(
            tiles.at[d], tile_parts.at[my_row], tile_send.at[j], tile_recv.at[my_row], d
        )

    def slice_copy(s, t, send):
        return to_col(pack.at[core, s], pack.at[core, s], send, slice_recv.at[s], t * 2 + core)

    def part_copy(j):
        d = other(j)
        return to_row(
            picked.at[pl.ds(d * chunk, chunk)],
            parts.at[my_row],
            part_send.at[j],
            part_recv.at[my_row],
            d,
        )

    def top_copy(d):
        return to_row(
            a_buf.at[pl.ds(top_start(d), chunk), :], olds.at[d], top_send.at[d], top_recv, d
        )

    def ring_copy(j, table, send, recv):
        return to_row(table.at[my_row], table.at[my_row], send.at[j], recv.at[my_row], other(j))

    def arrive(j, table, send, recv):
        s = other(j)
        to_row(table.at[s], table.at[s], send.at[j], recv.at[s], s).wait_recv()

    def fan_copy(j):
        q = lax.rem(my_col + j, cols_dev)
        return to_col(
            tile_pair.at[core], tile_pair.at[core], fan_send.at[j], fan_recv.at[core], q
        )

    @pl.when(chip == 0)
    def _():
        for j in range(1, rows_dev):
            tile_copy(j).start()
        tile_parts[my_row] = tiles[my_row]
        for s in range(1, chips):
            slice_copy(s, s, slice_send.at[s]).start()

    for j in range(1, rows_dev):
        part_copy(j).start()
    parts[my_row] = picked[pl.ds(pl.multiple_of(my_row * chunk, chunk), chunk), :]
    for d in range(rows_dev):
        owner = d * chunk // NB

        @pl.when(my_row == owner)
        def _():
            if d == owner:
                olds[d] = a_buf[top_start(d) : top_start(d) + chunk, :]
            else:
                top_copy(d).start()

    @pl.when(chip == 0)
    def _():
        for j in range(1, rows_dev):
            arrive(j, tile_parts, tile_send, tile_recv)
        total = tile_parts[0]
        for s in range(1, rows_dev):
            total = total + tile_parts[s]
        tile_pair[core] = total
        for j in range(1, cols_dev):
            fan_copy(j).start()

    @pl.when(chip != 0)
    def _():
        slice_copy(chip, chip, slice_send.at[0]).wait_recv()

    for j in range(1, chips):
        t = lax.rem(chip + j, chips)

        @pl.when(t != 0)
        def _():
            slice_copy(chip, t, spread_send.at[j]).start()

    for j in range(1, rows_dev):
        arrive(j, parts, part_send, part_recv)
    total = parts[0]
    for s in range(1, rows_dev):
        total = total + parts[s]
    news[my_row] = total
    for j in range(1, rows_dev):
        ring_copy(j, news, new_send, new_recv).start()

    for c in range(2):

        @pl.when(my_col != c)
        def _():
            to_col(
                tile_pair.at[c], tile_pair.at[c], fan_send.at[0], fan_recv.at[c], c
            ).wait_recv()

    zero_tile = tile_pair[0]
    one_tile = tile_pair[1]
    leads[my_row, :chunk] = jnp.where(first_tile, zero_tile, pltpu.roll(one_tile, NB, 1))
    leads[my_row, chunk:] = jnp.where(first_tile, pltpu.roll(zero_tile, NB, 1), one_tile)
    for j in range(1, rows_dev):
        ring_copy(j, leads, lead_send, lead_recv).start()

    for d in range(rows_dev):
        if d != d * chunk // NB:

            @pl.when(my_row == d)
            def _():
                top_copy(d).wait_recv()

    for j in range(1, rows_dev):
        ring_copy(j, olds, old_send, old_recv).start()

    groups = min(4, chips)
    per = chips // groups

    def pair_copy(g, which):
        held = pack.at[which, pl.ds(g * per, per)]
        return to_col(held, held, pair_send.at[g], pair_recv.at[g], chip * 2 + 1 - core)

    for g in range(groups):

        @pl.when(chip != 0)
        def _():
            for s in range(g * per, (g + 1) * per):

                @pl.when(chip != s)
                def _():
                    slice_copy(s, chip, slice_send.at[0]).wait_recv()

        pair_copy(g, core).start()

    for g in range(groups):
        pair_copy(g, 1 - core).wait_recv()
        for s in range(g * per, (g + 1) * per):
            zero_pack = pack[0, s]
            one_pack = pack[1, s]
            low = slice(slice_rows * s, slice_rows * (s + 1))
            high = slice(half_rows + slice_rows * s, half_rows + slice_rows * (s + 1))
            panel_ref[low, :] = jnp.where(first, zero_pack, one_pack)
            panel_ref[high, :] = pltpu.roll(jnp.where(first, one_pack, zero_pack), NB, 1)

    for j in range(1, rows_dev):
        arrive(j, leads, lead_send, lead_recv)
        arrive(j, news, new_send, new_recv)
    for d in range(rows_dev):
        part = slice(chunk * d, chunk * (d + 1))
        lead_ref[part, :] = leads[d, :chunk]
        old_lead_ref[part, :] = leads[d, chunk:]
        new_ref[part, :] = news[d]
    for j in range(1, rows_dev):
        arrive(j, olds, old_send, old_recv)
    for d in range(rows_dev):
        old_ref[chunk * d : chunk * (d + 1), :] = olds[d]

    for j in range(1, rows_dev):
        part_copy(j).wait_send()
        ring_copy(j, news, new_send, new_recv).wait_send()
        ring_copy(j, olds, old_send, old_recv).wait_send()
        ring_copy(j, leads, lead_send, lead_recv).wait_send()
    for d in range(rows_dev):
        owner = d * chunk // NB
        if d != owner:

            @pl.when(my_row == owner)
            def _():
                top_copy(d).wait_send()

    @pl.when(chip == 0)
    def _():
        for j in range(1, rows_dev):
            tile_copy(j).wait_send()
        for s in range(1, chips):
            slice_copy(s, s, slice_send.at[s]).wait_send()
        for j in range(1, cols_dev):
            fan_copy(j).wait_send()

    for j in range(1, chips):
        t = lax.rem(chip + j, chips)

        @pl.when(t != 0)
        def _():
            slice_copy(chip, t, spread_send.at[j]).wait_send()

    for g in range(groups):
        pair_copy(g, core).wait_send()


def move(matrix, pivots):
    rows_dev = lax.axis_size("row")
    cols_dev = lax.axis_size("col")
    chips = cols_dev // 2
    chunk = TOP // rows_dev
    rows, cols = matrix.shape
    dma = pltpu.SemaphoreType.DMA
    f32 = jnp.float32
    vmem = pl.BlockSpec(memory_space=pltpu.VMEM)
    by_row = dma((rows_dev,))
    by_chip = dma((chips,))
    return pl.pallas_call(
        move_kernel,
        out_shape=[
            jax.ShapeDtypeStruct((rows, TOP), f32),
            jax.ShapeDtypeStruct((TOP, cols), f32),
            jax.ShapeDtypeStruct((TOP, cols), f32),
            jax.ShapeDtypeStruct((TOP, TOP), f32),
            jax.ShapeDtypeStruct((TOP, TOP), f32),
        ],
        in_specs=[
            pl.BlockSpec(memory_space=pltpu.SMEM),
            pl.BlockSpec(memory_space=pl.ANY),
        ],
        out_specs=[vmem] * 5,
        scratch_shapes=[
            pltpu.VMEM((rows, cols), f32),
            pltpu.VMEM((2, chips, rows // 2 // chips, TOP), f32),
            pltpu.VMEM((TOP, cols), f32),
            pltpu.VMEM((rows_dev, chunk, cols), f32),
            pltpu.VMEM((rows_dev, chunk, cols), f32),
            pltpu.VMEM((rows_dev, chunk, cols), f32),
            pltpu.VMEM((rows_dev, chunk, TOP), f32),
            pltpu.VMEM((rows_dev, chunk, TOP), f32),
            pltpu.VMEM((2, chunk, TOP), f32),
            pltpu.VMEM((rows_dev, 2 * chunk, TOP), f32),
            dma,
            by_chip,
            by_chip,
            by_chip,
            dma((4,)),
            dma((4,)),
            by_row,
            by_row,
            by_row,
            dma,
            by_row,
            by_row,
            by_row,
            by_row,
            by_row,
            by_row,
            dma((cols_dev,)),
            dma((2,)),
            by_row,
            by_row,
        ],
        compiler_params=pltpu.CompilerParams(collective_id=0, has_side_effects=True),
        name="move",
    )(pivots, matrix)


def shards(matrix, pivots):
    panel, new_top, old_top, lead, old_lead = move(matrix, pivots)
    return finish(matrix, panel, lead, new_top, old_top, old_lead, pivots)


def solution(mesh):
    placed = (P("row", "col"), P())
    return jax.shard_map(
        shards, mesh=mesh, in_specs=placed, out_specs=P("row", "col"), check_vma=False
    )
```

```python
import jax
import jax.numpy as jnp
from jax import lax
from jax.experimental import pallas as pl
from jax.experimental.pallas import tpu as pltpu
from jax.sharding import PartitionSpec as P

NB = 64
TOP = 2 * NB
SUB = 8
CHUNKS = 8
PLACES = 8
HIGHEST = lax.Precision.HIGHEST
MESH = pl.DeviceIdType.MESH


def dot(a, b):
    return lax.dot_general(
        a, b, (((1,), (0,)), ((), ())), precision=HIGHEST, preferred_element_type=jnp.float32
    )


def place_of(pivot_ref, k):
    grid_rows = lax.axis_size("row")
    bits = NB.bit_length() - 1
    pivot = pivot_ref[k >> bits, k & (NB - 1)]
    local = (pivot >> (bits + grid_rows.bit_length() - 1) << bits) + (pivot & (NB - 1))
    mine = (pivot >> bits & (grid_rows - 1)) == lax.axis_index("row")
    return jnp.where(mine, local, -1)


def halves(x):
    high = x.astype(jnp.bfloat16)
    return high, (x - high.astype(jnp.float32)).astype(jnp.bfloat16)


def dot_pair(a, b):
    return lax.dot_general(
        a, b, (((1,), (0,)), ((), ())), preferred_element_type=jnp.float32
    )


def spread(block, lane):
    return jnp.broadcast_to(block[:, lane : lane + 1], block.shape)


def line(block, row):
    return jnp.broadcast_to(block[row : row + 1, :], block.shape)


def factor(a_ref, lu_ref, linv_ref, uinv_ref):
    n = TOP // SUB
    lane = lax.broadcasted_iota(jnp.int32, (SUB, TOP), 1)
    sub = lax.broadcasted_iota(jnp.int32, (SUB, TOP), 0)
    a = [a_ref[SUB * i : SUB * (i + 1), :] for i in range(n)]
    low = [jnp.where(lane == sub + SUB * i, 1.0, 0.0).astype(jnp.float32) for i in range(n)]
    upp = list(low)
    weights = jnp.ones((SUB, TOP), jnp.float32)
    for b in range(n):
        first = SUB * b
        cols = [spread(a[b], first + j) for j in range(SUB)]
        weight, entry, a_line, low_line = [], [], [], []
        for k in range(SUB):
            weight.append(1.0 / line(cols[k], k))
            weights = jnp.where(lane == first + k, weight[k], weights)
            entry.append([line(cols[j], k) if j > k else None for j in range(SUB)])
            a_line.append(jnp.where(lane > first + k, line(a[b], k), 0.0))
            low_line.append(line(low[b], k))
            if k < SUB - 1:
                multiplier = jnp.where(sub > k, cols[k] * weight[k], 0.0)
                for j in range(k + 1, SUB):
                    cols[j] = cols[j] - multiplier * entry[k][j]
                a[b] = a[b] - multiplier * a_line[k]
                low[b] = low[b] - multiplier * low_line[k]

        def multipliers(cols):
            cols = list(cols)
            for k in range(SUB):
                cols[k] = cols[k] * weight[k]
                for j in range(k + 1, SUB):
                    cols[j] = cols[j] - cols[k] * entry[k][j]
            return cols

        for i in range(b + 1, n):
            part = multipliers([spread(a[i], first + j) for j in range(SUB)])
            for k in range(SUB):
                a[i] = a[i] - part[k] * a_line[k]
                low[i] = low[i] - part[k] * low_line[k]
        for i in range(b + 1):
            if i == b:
                part = [jnp.where(sub == j, 1.0, 0.0).astype(jnp.float32) for j in range(SUB)]
            else:
                part = [spread(upp[i], first + j) for j in range(SUB)]
            part = multipliers(part)
            for k in range(SUB):
                upp[i] = upp[i] - part[k] * a_line[k]
    for i in range(n):
        part = slice(SUB * i, SUB * (i + 1))
        lu_ref[part, :] = jnp.where(sub + SUB * i > lane, a[i] * weights, a[i])
        linv_ref[part, :] = low[i]
        uinv_ref[part, :] = upp[i] * weights


def finish_kernel(
    pivot_ref,
    a_ref,
    panel_ref,
    lead_ref,
    new_top_ref,
    old_top_ref,
    old_lead_ref,
    out_ref,
    a_buf,
    p_buf,
    lu,
    linv,
    uinv,
    upper,
    solved,
    top_rows,
    in_sem,
    panel_sem,
    out_sem,
):
    my_row = lax.axis_index("row")
    my_col = lax.axis_index("col")
    rows = a_buf.shape[0] // CHUNKS
    copies = [
        pltpu.make_async_copy(
            a_ref.at[pl.ds(rows * i, rows)], a_buf.at[pl.ds(rows * i, rows)], in_sem.at[i]
        )
        for i in range(CHUNKS)
    ]
    panel_copy = pltpu.make_async_copy(panel_ref, p_buf, panel_sem)
    panel_copy.start()
    for copy in copies:
        copy.start()
    factor(lead_ref, lu, linv, uinv)
    upper[...] = dot(linv[...], new_top_ref[...])
    solved[...] = dot(uinv[...], upper[...])
    holds = my_col < 2
    own_lanes = (lax.broadcasted_iota(jnp.int32, (TOP, TOP), 1) < NB) & holds
    inverse = uinv[...]
    own = jnp.where(my_col == 0, inverse, pltpu.roll(inverse, NB, 1))
    solved[:, :TOP] = jnp.where(own_lanes, -own, solved[:, :TOP])
    top = pl.ds(pl.multiple_of(jnp.minimum(my_row, 1) * NB, NB), NB)
    corner = lu[top, :]
    corner = jnp.where(my_col == 0, corner, pltpu.roll(corner, NB, 1))
    top_rows[...] = upper[top, :]
    top_rows[:, :TOP] = jnp.where(own_lanes[:NB], corner, top_rows[:, :TOP])
    high, rest = halves(solved[...])
    twice = jnp.concatenate([high, high], axis=0)
    panel_copy.wait()
    for copy in copies:
        copy.wait()

    def place(step, carry):
        for j in range(PLACES):
            k = step * PLACES + j
            index = place_of(pivot_ref, k)

            @pl.when(index >= 0)
            def _():
                a_buf[pl.ds(index, 1), :] = old_top_ref[pl.ds(k, 1), :]
                p_buf[pl.ds(index, 1), :] = old_lead_ref[pl.ds(k, 1), :]

        return carry

    lax.fori_loop(0, TOP // PLACES, place, 0)
    dropped = (lax.broadcasted_iota(jnp.int32, (rows, a_buf.shape[1]), 1) < NB) & holds
    outs = []
    for i in range(CHUNKS):
        part = pl.ds(rows * i, rows)
        kept = jnp.where(dropped, 0.0, a_buf[part, :])
        left, left_rest = halves(p_buf[part, :])
        product = dot_pair(jnp.concatenate([left, left_rest], axis=1), twice)
        a_buf[part, :] = kept - (product + dot_pair(left, rest))
        if i == 0:

            @pl.when(my_row < 2)
            def _():
                a_buf[:NB, :] = top_rows[...]

        out = pltpu.make_async_copy(a_buf.at[part], out_ref.at[part], out_sem.at[i])
        out.start()
        outs.append(out)
    for out in outs:
        out.wait()


def finish(matrix, panel, lead, new_top, old_top, old_lead, pivots):
    any_spec = pl.BlockSpec(memory_space=pl.ANY)
    vmem = pl.BlockSpec(memory_space=pltpu.VMEM)
    return pl.pallas_call(
        finish_kernel,
        out_shape=jax.ShapeDtypeStruct(matrix.shape, jnp.float32),
        in_specs=[pl.BlockSpec(memory_space=pltpu.SMEM), any_spec, any_spec] + [vmem] * 4,
        out_specs=any_spec,
        scratch_shapes=[
            pltpu.VMEM(matrix.shape, jnp.float32),
            pltpu.VMEM(panel.shape, jnp.float32),
            pltpu.VMEM((TOP, TOP), jnp.float32),
            pltpu.VMEM((TOP, TOP), jnp.float32),
            pltpu.VMEM((TOP, TOP), jnp.float32),
            pltpu.VMEM(new_top.shape, jnp.float32),
            pltpu.VMEM(new_top.shape, jnp.float32),
            pltpu.VMEM((NB, new_top.shape[1]), jnp.float32),
            pltpu.SemaphoreType.DMA((CHUNKS,)),
            pltpu.SemaphoreType.DMA,
            pltpu.SemaphoreType.DMA((CHUNKS,)),
        ],
        name="finish",
    )(pivots, matrix, panel, lead, new_top, old_top, old_lead)


def move_kernel(
    pivot_ref,
    a_ref,
    panel_ref,
    new_ref,
    old_ref,
    lead_ref,
    old_lead_ref,
    a_buf,
    lead_buf,
    picked_lead,
    pack,
    picked,
    parts,
    news,
    olds,
    tiles,
    tile_parts,
    tile_pair,
    leads,
    load_sem,
    slice_send,
    slice_recv,
    spread_send,
    pair_send,
    pair_recv,
    part_send,
    part_recv,
    top_send,
    top_recv,
    new_send,
    new_recv,
    old_send,
    old_recv,
    tile_send,
    tile_recv,
    fan_send,
    fan_recv,
    lead_send,
    lead_recv,
):
    rows_dev = lax.axis_size("row")
    cols_dev = lax.axis_size("col")
    chips = cols_dev // 2
    my_row = lax.axis_index("row")
    my_col = lax.axis_index("col")
    chip = my_col // 2
    core = my_col % 2
    chunk = TOP // rows_dev
    half_rows = a_buf.shape[0] // 2
    slice_rows = half_rows // chips

    load_lead = pltpu.make_async_copy(a_ref.at[:, pl.ds(0, TOP)], lead_buf, load_sem.at[0])
    load = pltpu.make_async_copy(a_ref, a_buf, load_sem.at[1])

    @pl.when(chip == 0)
    def _():
        load_lead.start()

    load.start()
    barrier = pltpu.get_barrier_semaphore()
    for j in range(1, rows_dev):
        pl.semaphore_signal(
            barrier, inc=1, device_id={"row": lax.rem(my_row + j, rows_dev)}, device_id_type=MESH
        )
    for j in range(1, cols_dev):
        pl.semaphore_signal(
            barrier, inc=1, device_id={"col": lax.rem(my_col + j, cols_dev)}, device_id_type=MESH
        )

    def pick(table, target):
        def body(step, carry):
            for j in range(PLACES):
                k = step * PLACES + j
                index = place_of(pivot_ref, k)
                row = table[pl.ds(jnp.maximum(index, 0), 1), :]
                target[pl.ds(k, 1), :] = jnp.where(index >= 0, row, 0.0)
            return carry

        lax.fori_loop(0, TOP // PLACES, body, 0)

    first = lax.broadcasted_iota(jnp.int32, (slice_rows, TOP), 1) < NB
    first_tile = lax.broadcasted_iota(jnp.int32, (chunk, TOP), 1) < NB

    def top_start(d):
        return d * chunk - d * chunk // NB * NB

    @pl.when(chip == 0)
    def _():
        load_lead.wait()
        pick(lead_buf, picked_lead)
        for d in range(rows_dev):
            start = top_start(d)
            top = pltpu.roll(lead_buf[start : start + chunk, :], NB, 1)
            top = jnp.where(my_row == d * chunk // NB, top, 0.0)
            tiles[d] = jnp.where(first_tile, picked_lead[chunk * d : chunk * (d + 1), :], top)

    @pl.when(chip != 0)
    def _():
        load.wait()
        pick(a_buf, picked)

    pl.semaphore_wait(barrier, rows_dev + cols_dev - 2)

    def to_row(source, target, send, recv, d):
        return pltpu.make_async_remote_copy(
            src_ref=source,
            dst_ref=target,
            send_sem=send,
            recv_sem=recv,
            device_id={"row": d},
            device_id_type=MESH,
        )

    def to_col(source, target, send, recv, q):
        return pltpu.make_async_remote_copy(
            src_ref=source,
            dst_ref=target,
            send_sem=send,
            recv_sem=recv,
            device_id={"col": q},
            device_id_type=MESH,
        )

    def other(j):
        return lax.rem(my_row + j, rows_dev)

    def tile_copy(j):
        d = other(j)
        return to_row(
            tiles.at[d], tile_parts.at[my_row], tile_send.at[j], tile_recv.at[my_row], d
        )

    def slice_copy(s, t, send):
        return to_col(pack.at[core, s], pack.at[core, s], send, slice_recv.at[s], t * 2 + core)

    def part_copy(j):
        d = other(j)
        return to_row(
            picked.at[pl.ds(d * chunk, chunk)],
            parts.at[my_row],
            part_send.at[j],
            part_recv.at[my_row],
            d,
        )

    def top_copy(d):
        return to_row(
            a_buf.at[pl.ds(top_start(d), chunk), :], olds.at[d], top_send.at[d], top_recv, d
        )

    def ring_copy(j, table, send, recv):
        return to_row(table.at[my_row], table.at[my_row], send.at[j], recv.at[my_row], other(j))

    def arrive(j, table, send, recv):
        s = other(j)
        to_row(table.at[s], table.at[s], send.at[j], recv.at[s], s).wait_recv()

    two_stage = rows_dev == 8

    def hop(table, slot, part, d, send, recv):
        return to_row(table.at[slot, part], table.at[slot, part], send, recv, d)

    def stage_one(table, send, recv):
        return [
            hop(table, my_row, pl.ds(0, chunk), other(j), send.at[j], recv.at[my_row])
            for j in ((2, 6) if two_stage else range(1, rows_dev))
        ]

    def stage_two(table, send, recv):
        if not two_stage:
            return []
        whole = pl.ds(0, chunk)
        below, above = other(6), other(2)
        return [
            hop(table, below, whole, other(7), send.at[0], recv.at[below]),
            hop(table, below, whole, other(1), send.at[1], recv.at[below]),
            hop(table, below, pl.ds(0, chunk // 2), other(2), send.at[3], recv.at[below]),
            hop(table, above, whole, other(1), send.at[4], recv.at[above]),
            hop(table, above, whole, other(7), send.at[5], recv.at[above]),
            hop(
                table,
                above,
                pl.ds(chunk // 2, chunk // 2),
                other(6),
                send.at[7],
                recv.at[rows_dev],
            ),
        ]

    def begin(table, send, recv):
        for copy in stage_one(table, send, recv):
            copy.start()

    def forward(table, send, recv):
        if two_stage:
            arrive(6, table, send, recv)
            arrive(2, table, send, recv)
        for copy in stage_two(table, send, recv):
            copy.start()

    def gathered(table, send, recv):
        if not two_stage:
            for j in range(1, rows_dev):
                arrive(j, table, send, recv)
            return
        for j in (1, 3, 5, 7):
            arrive(j, table, send, recv)
        far = other(4)
        half = chunk // 2
        hop(table, far, pl.ds(0, half), far, send.at[0], recv.at[far]).wait_recv()
        hop(table, far, pl.ds(half, half), far, send.at[0], recv.at[rows_dev]).wait_recv()

    def sent(table, send, recv):
        for copy in stage_one(table, send, recv) + stage_two(table, send, recv):
            copy.wait_send()

    def fan_copy(j):
        q = lax.rem(my_col + j, cols_dev)
        return to_col(
            tile_pair.at[core], tile_pair.at[core], fan_send.at[j], fan_recv.at[core], q
        )

    @pl.when(chip == 0)
    def _():
        for j in range(1, rows_dev):
            tile_copy(j).start()
        tile_parts[my_row] = tiles[my_row]
        for s in range(chips):
            low = lead_buf[slice_rows * s : slice_rows * (s + 1), :]
            high = lead_buf[half_rows + slice_rows * s : half_rows + slice_rows * (s + 1), :]
            at_zero = jnp.where(core == 0, low, high)
            shifted = jnp.where(core == 0, high, low)
            pack[core, s] = jnp.where(first, at_zero, pltpu.roll(shifted, NB, 1))
        for s in range(1, chips):
            slice_copy(s, s, slice_send.at[s]).start()
        load.wait()
        pick(a_buf, picked)

    for j in range(1, rows_dev):
        part_copy(j).start()
    parts[my_row] = picked[pl.ds(pl.multiple_of(my_row * chunk, chunk), chunk), :]
    for d in range(rows_dev):
        owner = d * chunk // NB

        @pl.when(my_row == owner)
        def _():
            if d == owner:
                olds[d] = a_buf[top_start(d) : top_start(d) + chunk, :]
            else:
                top_copy(d).start()

    @pl.when(chip == 0)
    def _():
        for j in range(1, rows_dev):
            arrive(j, tile_parts, tile_send, tile_recv)
        total = tile_parts[0]
        for s in range(1, rows_dev):
            total = total + tile_parts[s]
        tile_pair[core] = total
        for j in range(1, cols_dev):
            fan_copy(j).start()

    @pl.when(chip != 0)
    def _():
        slice_copy(chip, chip, slice_send.at[0]).wait_recv()

    for j in range(1, chips):
        t = lax.rem(chip + j, chips)

        @pl.when(t != 0)
        def _():
            slice_copy(chip, t, spread_send.at[j]).start()

    for d in range(rows_dev):
        if d != d * chunk // NB:

            @pl.when(my_row == d)
            def _():
                top_copy(d).wait_recv()

    begin(olds, old_send, old_recv)
    for j in range(1, rows_dev):
        arrive(j, parts, part_send, part_recv)
    total = parts[0]
    for s in range(1, rows_dev):
        total = total + parts[s]
    news[my_row] = total
    begin(news, new_send, new_recv)
    forward(olds, old_send, old_recv)

    for c in range(2):

        @pl.when(my_col != c)
        def _():
            to_col(
                tile_pair.at[c], tile_pair.at[c], fan_send.at[0], fan_recv.at[c], c
            ).wait_recv()

    zero_tile = tile_pair[0]
    one_tile = tile_pair[1]
    leads[my_row, :chunk] = jnp.where(first_tile, zero_tile, pltpu.roll(one_tile, NB, 1))
    leads[my_row, chunk:] = jnp.where(first_tile, pltpu.roll(zero_tile, NB, 1), one_tile)
    for j in range(1, rows_dev):
        ring_copy(j, leads, lead_send, lead_recv).start()
    forward(news, new_send, new_recv)

    groups = min(4, chips)
    per = chips // groups

    def pair_copy(g, which):
        held = pack.at[which, pl.ds(g * per, per)]
        return to_col(held, held, pair_send.at[g], pair_recv.at[g], chip * 2 + 1 - core)

    for g in range(groups):

        @pl.when(chip != 0)
        def _():
            for s in range(g * per, (g + 1) * per):

                @pl.when(chip != s)
                def _():
                    slice_copy(s, chip, slice_send.at[0]).wait_recv()

        pair_copy(g, core).start()

    for g in range(groups):
        pair_copy(g, 1 - core).wait_recv()
        for s in range(g * per, (g + 1) * per):
            zero_pack = pack[0, s]
            one_pack = pack[1, s]
            low = slice(slice_rows * s, slice_rows * (s + 1))
            high = slice(half_rows + slice_rows * s, half_rows + slice_rows * (s + 1))
            panel_ref[low, :] = jnp.where(first, zero_pack, one_pack)
            panel_ref[high, :] = pltpu.roll(jnp.where(first, one_pack, zero_pack), NB, 1)

    for j in range(1, rows_dev):
        arrive(j, leads, lead_send, lead_recv)
    gathered(news, new_send, new_recv)
    for d in range(rows_dev):
        part = slice(chunk * d, chunk * (d + 1))
        lead_ref[part, :] = leads[d, :chunk]
        old_lead_ref[part, :] = leads[d, chunk:]
        new_ref[part, :] = news[d]
    gathered(olds, old_send, old_recv)
    for d in range(rows_dev):
        old_ref[chunk * d : chunk * (d + 1), :] = olds[d]

    for j in range(1, rows_dev):
        part_copy(j).wait_send()
        ring_copy(j, leads, lead_send, lead_recv).wait_send()
    sent(news, new_send, new_recv)
    sent(olds, old_send, old_recv)
    for d in range(rows_dev):
        owner = d * chunk // NB
        if d != owner:

            @pl.when(my_row == owner)
            def _():
                top_copy(d).wait_send()

    @pl.when(chip == 0)
    def _():
        for j in range(1, rows_dev):
            tile_copy(j).wait_send()
        for s in range(1, chips):
            slice_copy(s, s, slice_send.at[s]).wait_send()
        for j in range(1, cols_dev):
            fan_copy(j).wait_send()

    for j in range(1, chips):
        t = lax.rem(chip + j, chips)

        @pl.when(t != 0)
        def _():
            slice_copy(chip, t, spread_send.at[j]).wait_send()

    for g in range(groups):
        pair_copy(g, core).wait_send()


def move(matrix, pivots):
    rows_dev = lax.axis_size("row")
    cols_dev = lax.axis_size("col")
    chips = cols_dev // 2
    chunk = TOP // rows_dev
    rows, cols = matrix.shape
    dma = pltpu.SemaphoreType.DMA
    f32 = jnp.float32
    vmem = pl.BlockSpec(memory_space=pltpu.VMEM)
    by_row = dma((rows_dev,))
    by_chip = dma((chips,))
    return pl.pallas_call(
        move_kernel,
        out_shape=[
            jax.ShapeDtypeStruct((rows, TOP), f32),
            jax.ShapeDtypeStruct((TOP, cols), f32),
            jax.ShapeDtypeStruct((TOP, cols), f32),
            jax.ShapeDtypeStruct((TOP, TOP), f32),
            jax.ShapeDtypeStruct((TOP, TOP), f32),
        ],
        in_specs=[
            pl.BlockSpec(memory_space=pltpu.SMEM),
            pl.BlockSpec(memory_space=pl.ANY),
        ],
        out_specs=[vmem] * 5,
        scratch_shapes=[
            pltpu.VMEM((rows, cols), f32),
            pltpu.VMEM((rows, TOP), f32),
            pltpu.VMEM((TOP, TOP), f32),
            pltpu.VMEM((2, chips, rows // 2 // chips, TOP), f32),
            pltpu.VMEM((TOP, cols), f32),
            pltpu.VMEM((rows_dev, chunk, cols), f32),
            pltpu.VMEM((rows_dev, chunk, cols), f32),
            pltpu.VMEM((rows_dev, chunk, cols), f32),
            pltpu.VMEM((rows_dev, chunk, TOP), f32),
            pltpu.VMEM((rows_dev, chunk, TOP), f32),
            pltpu.VMEM((2, chunk, TOP), f32),
            pltpu.VMEM((rows_dev, 2 * chunk, TOP), f32),
            dma((2,)),
            by_chip,
            by_chip,
            by_chip,
            dma((4,)),
            dma((4,)),
            by_row,
            by_row,
            by_row,
            dma,
            by_row,
            dma((rows_dev + 1,)),
            by_row,
            dma((rows_dev + 1,)),
            by_row,
            by_row,
            dma((cols_dev,)),
            dma((2,)),
            by_row,
            by_row,
        ],
        compiler_params=pltpu.CompilerParams(collective_id=0, has_side_effects=True),
        name="move",
    )(pivots, matrix)


def shards(matrix, pivots):
    panel, new_top, old_top, lead, old_lead = move(matrix, pivots)
    return finish(matrix, panel, lead, new_top, old_top, old_lead, pivots)


def solution(mesh):
    placed = (P("row", "col"), P())
    return jax.shard_map(
        shards, mesh=mesh, in_specs=placed, out_specs=P("row", "col"), check_vma=False
    )
```

```python
import jax
import jax.numpy as jnp
from jax import lax
from jax.experimental import pallas as pl
from jax.experimental.pallas import tpu as pltpu
from jax.sharding import PartitionSpec as P

NB = 64
TOP = 2 * NB
SUB = 8
CHUNKS = 8
PLACES = 8
MESH = pl.DeviceIdType.MESH


def place_of(pivot_ref, k):
    grid_rows = lax.axis_size("row")
    bits = NB.bit_length() - 1
    pivot = pivot_ref[k >> bits, k & (NB - 1)]
    local = (pivot >> (bits + grid_rows.bit_length() - 1) << bits) + (pivot & (NB - 1))
    mine = (pivot >> bits & (grid_rows - 1)) == lax.axis_index("row")
    return jnp.where(mine, local, -1)


def halves(x):
    high = x.astype(jnp.bfloat16)
    return high, (x - high.astype(jnp.float32)).astype(jnp.bfloat16)


def dot_pair(a, b):
    return lax.dot_general(
        a, b, (((1,), (0,)), ((), ())), preferred_element_type=jnp.float32
    )


def dot(a, b):
    high, rest = halves(a)
    b_high, b_rest = halves(b)
    both = jnp.concatenate([high, rest], axis=1)
    return dot_pair(both, jnp.concatenate([b_high, b_high], axis=0)) + dot_pair(high, b_rest)


def spread(block, lane):
    return jnp.broadcast_to(block[:, lane : lane + 1], block.shape)


def line(block, row):
    return jnp.broadcast_to(block[row : row + 1, :], block.shape)


def factor(a_ref, lu_ref, linv_ref, uinv_ref):
    n = TOP // SUB
    lane = lax.broadcasted_iota(jnp.int32, (SUB, TOP), 1)
    sub = lax.broadcasted_iota(jnp.int32, (SUB, TOP), 0)
    chunk = a_ref.shape[1] // 2
    a = []
    for i in range(n):
        slot, start = divmod(SUB * i, chunk)
        a.append(a_ref[slot, start : start + SUB, :])
    low = [jnp.where(lane == sub + SUB * i, 1.0, 0.0).astype(jnp.float32) for i in range(n)]
    upp = list(low)
    weights = jnp.ones((SUB, TOP), jnp.float32)
    for b in range(n):
        first = SUB * b
        cols = [spread(a[b], first + j) for j in range(SUB)]
        weight, entry, a_line, low_line = [], [], [], []
        for k in range(SUB):
            weight.append(1.0 / line(cols[k], k))
            weights = jnp.where(lane == first + k, weight[k], weights)
            entry.append([line(cols[j], k) if j > k else None for j in range(SUB)])
            a_line.append(jnp.where(lane > first + k, line(a[b], k), 0.0))
            low_line.append(line(low[b], k))
            if k < SUB - 1:
                multiplier = jnp.where(sub > k, cols[k] * weight[k], 0.0)
                for j in range(k + 1, SUB):
                    cols[j] = cols[j] - multiplier * entry[k][j]
                a[b] = a[b] - multiplier * a_line[k]
                low[b] = low[b] - multiplier * low_line[k]

        def multipliers(cols):
            cols = list(cols)
            for k in range(SUB):
                cols[k] = cols[k] * weight[k]
                for j in range(k + 1, SUB):
                    cols[j] = cols[j] - cols[k] * entry[k][j]
            return cols

        for i in range(b + 1, n):
            part = multipliers([spread(a[i], first + j) for j in range(SUB)])
            for k in range(SUB):
                a[i] = a[i] - part[k] * a_line[k]
                low[i] = low[i] - part[k] * low_line[k]
        for i in range(b + 1):
            if i == b:
                part = [jnp.where(sub == j, 1.0, 0.0).astype(jnp.float32) for j in range(SUB)]
            else:
                part = [spread(upp[i], first + j) for j in range(SUB)]
            part = multipliers(part)
            for k in range(SUB):
                upp[i] = upp[i] - part[k] * a_line[k]
    for i in range(n):
        part = slice(SUB * i, SUB * (i + 1))
        lu_ref[part, :] = jnp.where(sub + SUB * i > lane, a[i] * weights, a[i])
        linv_ref[part, :] = low[i]
        uinv_ref[part, :] = upp[i] * weights


def finish_kernel(
    pivot_ref,
    a_ref,
    panel_ref,
    leads_ref,
    news_ref,
    olds_ref,
    out_ref,
    a_buf,
    p_buf,
    news,
    olds,
    lu,
    linv,
    uinv,
    upper,
    solved,
    top_rows,
    in_sem,
    side_sem,
    out_sem,
):
    my_row = lax.axis_index("row")
    my_col = lax.axis_index("col")
    rows = a_buf.shape[0] // CHUNKS
    copies = [
        pltpu.make_async_copy(
            a_ref.at[pl.ds(rows * i, rows)], a_buf.at[pl.ds(rows * i, rows)], in_sem.at[i]
        )
        for i in range(CHUNKS)
    ]
    news_copy = pltpu.make_async_copy(news_ref, news, side_sem.at[0])
    olds_copy = pltpu.make_async_copy(olds_ref, olds, side_sem.at[1])
    panel_copy = pltpu.make_async_copy(panel_ref, p_buf, side_sem.at[2])
    for copy in (news_copy, olds_copy, panel_copy):
        copy.start()
    for copy in copies:
        copy.start()
    factor(leads_ref, lu, linv, uinv)
    news_copy.wait()
    upper[...] = dot(linv[...], news[...].reshape(upper.shape))
    solved[...] = dot(uinv[...], upper[...])
    holds = my_col < 2
    own_lanes = (lax.broadcasted_iota(jnp.int32, (TOP, TOP), 1) < NB) & holds
    inverse = uinv[...]
    own = jnp.where(my_col == 0, inverse, pltpu.roll(inverse, NB, 1))
    solved[:, :TOP] = jnp.where(own_lanes, -own, solved[:, :TOP])
    top = pl.ds(pl.multiple_of(jnp.minimum(my_row, 1) * NB, NB), NB)
    corner = lu[top, :]
    corner = jnp.where(my_col == 0, corner, pltpu.roll(corner, NB, 1))
    top_rows[...] = upper[top, :]
    top_rows[:, :TOP] = jnp.where(own_lanes[:NB], corner, top_rows[:, :TOP])
    high, rest = halves(solved[...])
    twice = jnp.concatenate([high, high], axis=0)
    olds_copy.wait()
    panel_copy.wait()
    for copy in copies:
        copy.wait()

    chunk = olds.shape[1]
    bits = chunk.bit_length() - 1

    def place(step, carry):
        for j in range(PLACES):
            k = step * PLACES + j
            index = place_of(pivot_ref, k)

            @pl.when(index >= 0)
            def _():
                slot = k >> bits
                row = k & (chunk - 1)
                a_buf[pl.ds(index, 1), :] = olds[slot, pl.ds(row, 1), :]
                p_buf[pl.ds(index, 1), :] = leads_ref[slot, pl.ds(chunk + row, 1), :]

        return carry

    lax.fori_loop(0, TOP // PLACES, place, 0)
    dropped = (lax.broadcasted_iota(jnp.int32, (rows, a_buf.shape[1]), 1) < NB) & holds
    outs = []
    for i in range(CHUNKS):
        part = pl.ds(rows * i, rows)
        kept = jnp.where(dropped, 0.0, a_buf[part, :])
        left, left_rest = halves(p_buf[part, :])
        product = dot_pair(jnp.concatenate([left, left_rest], axis=1), twice)
        a_buf[part, :] = kept - (product + dot_pair(left, rest))
        if i == 0:

            @pl.when(my_row < 2)
            def _():
                a_buf[:NB, :] = top_rows[...]

        out = pltpu.make_async_copy(a_buf.at[part], out_ref.at[part], out_sem.at[i])
        out.start()
        outs.append(out)
    for out in outs:
        out.wait()


def finish(matrix, panel, leads, news, olds, pivots):
    any_spec = pl.BlockSpec(memory_space=pl.ANY)
    vmem = pl.BlockSpec(memory_space=pltpu.VMEM)
    return pl.pallas_call(
        finish_kernel,
        out_shape=jax.ShapeDtypeStruct(matrix.shape, jnp.float32),
        in_specs=[pl.BlockSpec(memory_space=pltpu.SMEM), any_spec, any_spec, vmem, any_spec, any_spec],
        out_specs=any_spec,
        scratch_shapes=[
            pltpu.VMEM(matrix.shape, jnp.float32),
            pltpu.VMEM(panel.shape, jnp.float32),
            pltpu.VMEM(news.shape, jnp.float32),
            pltpu.VMEM(olds.shape, jnp.float32),
            pltpu.VMEM((TOP, TOP), jnp.float32),
            pltpu.VMEM((TOP, TOP), jnp.float32),
            pltpu.VMEM((TOP, TOP), jnp.float32),
            pltpu.VMEM((TOP, matrix.shape[1]), jnp.float32),
            pltpu.VMEM((TOP, matrix.shape[1]), jnp.float32),
            pltpu.VMEM((NB, matrix.shape[1]), jnp.float32),
            pltpu.SemaphoreType.DMA((CHUNKS,)),
            pltpu.SemaphoreType.DMA((3,)),
            pltpu.SemaphoreType.DMA((CHUNKS,)),
        ],
        name="finish",
    )(pivots, matrix, panel, leads, news, olds)


def move_kernel(
    pivot_ref,
    a_ref,
    panel_ref,
    leads_ref,
    news_ref,
    olds_ref,
    a_buf,
    lead_buf,
    picked_lead,
    pack,
    picked,
    parts,
    news,
    olds,
    tiles,
    tile_parts,
    tile_pair,
    leads,
    sums,
    panel,
    load_sem,
    slice_send,
    slice_recv,
    spread_send,
    pair_send,
    pair_recv,
    part_send,
    part_recv,
    top_send,
    top_recv,
    new_send,
    new_recv,
    old_send,
    old_recv,
    tile_send,
    tile_recv,
    fan_send,
    fan_recv,
    lead_send,
    lead_recv,
    panel_out,
    side_out,
):
    rows_dev = lax.axis_size("row")
    cols_dev = lax.axis_size("col")
    chips = cols_dev // 2
    my_row = lax.axis_index("row")
    my_col = lax.axis_index("col")
    chip = my_col // 2
    core = my_col % 2
    chunk = TOP // rows_dev
    half_rows = a_buf.shape[0] // 2
    slice_rows = half_rows // chips

    load_lead = pltpu.make_async_copy(a_ref.at[:, pl.ds(0, TOP)], lead_buf, load_sem.at[0])
    load = pltpu.make_async_copy(a_ref, a_buf, load_sem.at[1])

    @pl.when(chip == 0)
    def _():
        load_lead.start()

    load.start()
    barrier = pltpu.get_barrier_semaphore()
    for j in range(1, rows_dev):
        pl.semaphore_signal(
            barrier, inc=1, device_id={"row": lax.rem(my_row + j, rows_dev)}, device_id_type=MESH
        )
    for j in range(1, cols_dev):
        pl.semaphore_signal(
            barrier, inc=1, device_id={"col": lax.rem(my_col + j, cols_dev)}, device_id_type=MESH
        )

    def pick(table, target):
        def body(step, carry):
            for j in range(PLACES):
                k = step * PLACES + j
                index = place_of(pivot_ref, k)
                row = table[pl.ds(jnp.maximum(index, 0), 1), :]
                target[pl.ds(k, 1), :] = jnp.where(index >= 0, row, 0.0)
            return carry

        lax.fori_loop(0, TOP // PLACES, body, 0)

    first = lax.broadcasted_iota(jnp.int32, (slice_rows, TOP), 1) < NB
    first_tile = lax.broadcasted_iota(jnp.int32, (chunk, TOP), 1) < NB

    def top_start(d):
        return d * chunk - d * chunk // NB * NB

    @pl.when(chip == 0)
    def _():
        load_lead.wait()
        pick(lead_buf, picked_lead)
        for d in range(rows_dev):
            start = top_start(d)
            top = pltpu.roll(lead_buf[start : start + chunk, :], NB, 1)
            top = jnp.where(my_row == d * chunk // NB, top, 0.0)
            tiles[d] = jnp.where(first_tile, picked_lead[chunk * d : chunk * (d + 1), :], top)

    @pl.when(chip != 0)
    def _():
        load.wait()
        pick(a_buf, picked)

    pl.semaphore_wait(barrier, rows_dev + cols_dev - 2)

    def to_row(source, target, send, recv, d):
        return pltpu.make_async_remote_copy(
            src_ref=source,
            dst_ref=target,
            send_sem=send,
            recv_sem=recv,
            device_id={"row": d},
            device_id_type=MESH,
        )

    def to_col(source, target, send, recv, q):
        return pltpu.make_async_remote_copy(
            src_ref=source,
            dst_ref=target,
            send_sem=send,
            recv_sem=recv,
            device_id={"col": q},
            device_id_type=MESH,
        )

    def other(j):
        return lax.rem(my_row + j, rows_dev)

    def tile_copy(j):
        d = other(j)
        return to_row(
            tiles.at[d], tile_parts.at[my_row], tile_send.at[j], tile_recv.at[my_row], d
        )

    def slice_copy(s, t, send):
        return to_col(pack.at[core, s], pack.at[core, s], send, slice_recv.at[s], t * 2 + core)

    half = chunk // 2
    all_rows = pl.ds(0, chunk)

    def part_of(d, part=None):
        start, size = (0, chunk) if part is None else (part * half, half)
        return picked.at[pl.ds(d * chunk + start, size)]

    def part_copy(slot, target, relay, part=None):
        rows = all_rows if part is None else pl.ds(part * half, half)
        return to_row(
            part_of(other(target), part),
            parts.at[slot, rows],
            part_send.at[slot],
            part_recv.at[slot],
            other(relay),
        )

    def part_copies():
        return [
            part_copy(0, 7, 1),
            part_copy(1, 5, 7),
            part_copy(2, 4, 6, 0),
            part_copy(3, 1, 7),
            part_copy(4, 3, 1),
            part_copy(5, 4, 2, 1),
        ]

    def sum_copy(which, target):
        slot = 6 + which
        return to_row(
            sums.at[which], parts.at[slot], part_send.at[slot], part_recv.at[slot], other(target)
        )

    def value_of(d):
        return picked[pl.ds(pl.multiple_of(d * chunk, chunk), chunk), :]

    def top_copy(d):
        return to_row(
            a_buf.at[pl.ds(top_start(d), chunk), :], olds.at[d], top_send.at[d], top_recv, d
        )

    def ring_copy(j, table, send, recv):
        return to_row(table.at[my_row], table.at[my_row], send.at[j], recv.at[my_row], other(j))

    def arrive(j, table, send, recv):
        s = other(j)
        to_row(table.at[s], table.at[s], send.at[j], recv.at[s], s).wait_recv()

    def hop(table, slot, part, d, send, recv):
        return to_row(table.at[slot, part], table.at[slot, part], send, recv, d)

    def stage_one(table, send, recv):
        return [
            hop(table, my_row, all_rows, other(j), send.at[j], recv.at[my_row]) for j in (2, 6)
        ]

    def stage_two(table, send, recv):
        below, above = other(6), other(2)
        upper = pl.ds(0, half)
        lower = pl.ds(half, half)
        return [
            hop(table, below, all_rows, other(7), send.at[0], recv.at[below]),
            hop(table, below, all_rows, other(1), send.at[1], recv.at[below]),
            hop(table, below, upper, other(2), send.at[3], recv.at[below]),
            hop(table, above, all_rows, other(1), send.at[4], recv.at[above]),
            hop(table, above, all_rows, other(7), send.at[5], recv.at[above]),
            hop(table, above, lower, other(6), send.at[7], recv.at[rows_dev]),
        ]

    def begin(table, send, recv):
        for copy in stage_one(table, send, recv):
            copy.start()

    def forward(table, send, recv):
        arrive(6, table, send, recv)
        arrive(2, table, send, recv)
        for copy in stage_two(table, send, recv):
            copy.start()

    def gathered(table, send, recv):
        for j in (1, 3, 5, 7):
            arrive(j, table, send, recv)
        far = other(4)
        hop(table, far, pl.ds(0, half), far, send.at[0], recv.at[far]).wait_recv()
        hop(table, far, pl.ds(half, half), far, send.at[0], recv.at[rows_dev]).wait_recv()

    def sent(table, send, recv):
        for copy in stage_one(table, send, recv) + stage_two(table, send, recv):
            copy.wait_send()

    def fan_copy(j):
        q = lax.rem(my_col + j, cols_dev)
        return to_col(
            tile_pair.at[core], tile_pair.at[core], fan_send.at[j], fan_recv.at[core], q
        )

    @pl.when(chip == 0)
    def _():
        for j in range(1, rows_dev):
            tile_copy(j).start()
        tile_parts[my_row] = tiles[my_row]
        for s in range(chips):
            low = lead_buf[slice_rows * s : slice_rows * (s + 1), :]
            high = lead_buf[half_rows + slice_rows * s : half_rows + slice_rows * (s + 1), :]
            at_zero = jnp.where(core == 0, low, high)
            shifted = jnp.where(core == 0, high, low)
            pack[core, s] = jnp.where(first, at_zero, pltpu.roll(shifted, NB, 1))
        for s in range(1, chips):
            slice_copy(s, s, slice_send.at[s]).start()
        load.wait()
        pick(a_buf, picked)

    for copy in part_copies():
        copy.start()
    for d in range(rows_dev):
        owner = d * chunk // NB

        @pl.when(my_row == owner)
        def _():
            if d == owner:
                olds[d] = a_buf[top_start(d) : top_start(d) + chunk, :]
            else:
                top_copy(d).start()

    @pl.when(chip == 0)
    def _():
        for j in range(1, rows_dev):
            arrive(j, tile_parts, tile_send, tile_recv)
        total = tile_parts[0]
        for s in range(1, rows_dev):
            total = total + tile_parts[s]
        tile_pair[core] = total
        for j in range(1, cols_dev):
            fan_copy(j).start()

    @pl.when(chip != 0)
    def _():
        slice_copy(chip, chip, slice_send.at[0]).wait_recv()

    for j in range(1, chips):
        t = lax.rem(chip + j, chips)

        @pl.when(t != 0)
        def _():
            slice_copy(chip, t, spread_send.at[j]).start()

    for d in range(rows_dev):
        if d != d * chunk // NB:

            @pl.when(my_row == d)
            def _():
                top_copy(d).wait_recv()

    begin(olds, old_send, old_recv)
    for copy in part_copies():
        copy.wait_recv()
    low_sum = value_of(other(6)) + parts[0] + parts[1]
    sums[0, :half] = low_sum[:half] + parts[2, :half]
    sums[0, half:] = low_sum[half:]
    high_sum = value_of(other(2)) + parts[3] + parts[4]
    sums[1, :half] = high_sum[:half]
    sums[1, half:] = high_sum[half:] + parts[5, half:]
    sum_copy(0, 6).start()
    sum_copy(1, 2).start()
    forward(olds, old_send, old_recv)
    sum_copy(0, 6).wait_recv()
    sum_copy(1, 2).wait_recv()
    news[my_row] = value_of(my_row) + parts[6] + parts[7]
    begin(news, new_send, new_recv)

    for c in range(2):

        @pl.when(my_col != c)
        def _():
            to_col(
                tile_pair.at[c], tile_pair.at[c], fan_send.at[0], fan_recv.at[c], c
            ).wait_recv()

    zero_tile = tile_pair[0]
    one_tile = tile_pair[1]
    leads[my_row, :chunk] = jnp.where(first_tile, zero_tile, pltpu.roll(one_tile, NB, 1))
    leads[my_row, chunk:] = jnp.where(first_tile, pltpu.roll(zero_tile, NB, 1), one_tile)
    for j in range(1, rows_dev):
        ring_copy(j, leads, lead_send, lead_recv).start()
    forward(news, new_send, new_recv)

    groups = min(4, chips)
    per = chips // groups

    def panel_copies(g):
        size = per * slice_rows
        copies = []
        for side in range(2):
            rows = pl.ds(side * half_rows + g * size, size)
            copies.append(
                pltpu.make_async_copy(panel.at[rows], panel_ref.at[rows], panel_out.at[2 * g + side])
            )
        return copies

    def pair_copy(g, which):
        held = pack.at[which, pl.ds(g * per, per)]
        return to_col(held, held, pair_send.at[g], pair_recv.at[g], chip * 2 + 1 - core)

    for g in range(groups):

        @pl.when(chip != 0)
        def _():
            for s in range(g * per, (g + 1) * per):

                @pl.when(chip != s)
                def _():
                    slice_copy(s, chip, slice_send.at[0]).wait_recv()

        pair_copy(g, core).start()

    for g in range(groups):
        pair_copy(g, 1 - core).wait_recv()
        for s in range(g * per, (g + 1) * per):
            zero_pack = pack[0, s]
            one_pack = pack[1, s]
            low = slice(slice_rows * s, slice_rows * (s + 1))
            high = slice(half_rows + slice_rows * s, half_rows + slice_rows * (s + 1))
            panel[low, :] = jnp.where(first, zero_pack, one_pack)
            panel[high, :] = pltpu.roll(jnp.where(first, one_pack, zero_pack), NB, 1)
        for copy in panel_copies(g):
            copy.start()

    side = [
        pltpu.make_async_copy(table, target, side_out.at[i])
        for i, (table, target) in enumerate(
            ((leads, leads_ref), (news, news_ref), (olds, olds_ref))
        )
    ]
    for j in range(1, rows_dev):
        arrive(j, leads, lead_send, lead_recv)
    side[0].start()
    gathered(olds, old_send, old_recv)
    side[2].start()
    gathered(news, new_send, new_recv)
    side[1].start()

    for copy in part_copies():
        copy.wait_send()
    sum_copy(0, 6).wait_send()
    sum_copy(1, 2).wait_send()
    for j in range(1, rows_dev):
        ring_copy(j, leads, lead_send, lead_recv).wait_send()
    sent(news, new_send, new_recv)
    sent(olds, old_send, old_recv)
    for d in range(rows_dev):
        owner = d * chunk // NB
        if d != owner:

            @pl.when(my_row == owner)
            def _():
                top_copy(d).wait_send()

    @pl.when(chip == 0)
    def _():
        for j in range(1, rows_dev):
            tile_copy(j).wait_send()
        for s in range(1, chips):
            slice_copy(s, s, slice_send.at[s]).wait_send()
        for j in range(1, cols_dev):
            fan_copy(j).wait_send()

    for j in range(1, chips):
        t = lax.rem(chip + j, chips)

        @pl.when(t != 0)
        def _():
            slice_copy(chip, t, spread_send.at[j]).wait_send()

    for g in range(groups):
        pair_copy(g, core).wait_send()
        for copy in panel_copies(g):
            copy.wait()
    for copy in side:
        copy.wait()


def move(matrix, pivots):
    rows_dev = lax.axis_size("row")
    cols_dev = lax.axis_size("col")
    chips = cols_dev // 2
    chunk = TOP // rows_dev
    rows, cols = matrix.shape
    dma = pltpu.SemaphoreType.DMA
    f32 = jnp.float32
    by_row = dma((rows_dev,))
    by_chip = dma((chips,))
    return pl.pallas_call(
        move_kernel,
        out_shape=[
            jax.ShapeDtypeStruct((rows, TOP), f32),
            jax.ShapeDtypeStruct((rows_dev, 2 * chunk, TOP), f32),
            jax.ShapeDtypeStruct((rows_dev, chunk, cols), f32),
            jax.ShapeDtypeStruct((rows_dev, chunk, cols), f32),
        ],
        in_specs=[
            pl.BlockSpec(memory_space=pltpu.SMEM),
            pl.BlockSpec(memory_space=pl.ANY),
        ],
        out_specs=[pl.BlockSpec(memory_space=pl.ANY)] * 4,
        scratch_shapes=[
            pltpu.VMEM((rows, cols), f32),
            pltpu.VMEM((rows, TOP), f32),
            pltpu.VMEM((TOP, TOP), f32),
            pltpu.VMEM((2, chips, rows // 2 // chips, TOP), f32),
            pltpu.VMEM((TOP, cols), f32),
            pltpu.VMEM((rows_dev, chunk, cols), f32),
            pltpu.VMEM((rows_dev, chunk, cols), f32),
            pltpu.VMEM((rows_dev, chunk, cols), f32),
            pltpu.VMEM((rows_dev, chunk, TOP), f32),
            pltpu.VMEM((rows_dev, chunk, TOP), f32),
            pltpu.VMEM((2, chunk, TOP), f32),
            pltpu.VMEM((rows_dev, 2 * chunk, TOP), f32),
            pltpu.VMEM((2, chunk, cols), f32),
            pltpu.VMEM((rows, TOP), f32),
            dma((2,)),
            by_chip,
            by_chip,
            by_chip,
            dma((4,)),
            dma((4,)),
            by_row,
            by_row,
            by_row,
            dma,
            by_row,
            dma((rows_dev + 1,)),
            by_row,
            dma((rows_dev + 1,)),
            by_row,
            by_row,
            dma((cols_dev,)),
            dma((2,)),
            by_row,
            by_row,
            dma((8,)),
            dma((3,)),
        ],
        compiler_params=pltpu.CompilerParams(collective_id=0, has_side_effects=True),
        name="move",
    )(pivots, matrix)


def shards(matrix, pivots):
    panel, leads, news, olds = move(matrix, pivots)
    return finish(matrix, panel, leads, news, olds, pivots)


def solution(mesh):
    placed = (P("row", "col"), P())
    return jax.shard_map(
        shards, mesh=mesh, in_specs=placed, out_specs=P("row", "col"), check_vma=False
    )
```

```python
import jax
import jax.numpy as jnp
from jax import lax
from jax.experimental import pallas as pl
from jax.experimental.pallas import tpu as pltpu
from jax.sharding import PartitionSpec as P

NB = 64
TOP = 2 * NB
SUB = 8
CHUNKS = 8
PLACES = 8
MESH = pl.DeviceIdType.MESH


def place_of(pivot_ref, k):
    grid_rows = lax.axis_size("row")
    bits = NB.bit_length() - 1
    pivot = pivot_ref[k >> bits, k & (NB - 1)]
    local = (pivot >> (bits + grid_rows.bit_length() - 1) << bits) + (pivot & (NB - 1))
    mine = (pivot >> bits & (grid_rows - 1)) == lax.axis_index("row")
    return jnp.where(mine, local, -1)


def halves(x):
    high = x.astype(jnp.bfloat16)
    return high, (x - high.astype(jnp.float32)).astype(jnp.bfloat16)


def dot_pair(a, b):
    return lax.dot_general(
        a, b, (((1,), (0,)), ((), ())), preferred_element_type=jnp.float32
    )


def dot(a, b):
    high, rest = halves(a)
    b_high, b_rest = halves(b)
    both = jnp.concatenate([high, rest], axis=1)
    return dot_pair(both, jnp.concatenate([b_high, b_high], axis=0)) + dot_pair(high, b_rest)


def spread(block, lane):
    return jnp.broadcast_to(block[:, lane : lane + 1], block.shape)


def line(block, row):
    return jnp.broadcast_to(block[row : row + 1, :], block.shape)


def factor(a_ref, lu_ref, linv_ref, uinv_ref):
    n = TOP // SUB
    chunk = a_ref.shape[1] // 2
    lane = lax.broadcasted_iota(jnp.int32, (SUB, TOP), 1)
    sub = lax.broadcasted_iota(jnp.int32, (SUB, TOP), 0)
    row_id = lax.broadcasted_iota(jnp.int32, (TOP, TOP), 0)
    lane_id = lax.broadcasted_iota(jnp.int32, (TOP, TOP), 1)
    rest = jnp.concatenate([a_ref[slot, :chunk] for slot in range(TOP // chunk)], axis=0)
    low_rest = jnp.where(row_id == lane_id, 1.0, 0.0).astype(jnp.float32)
    eye = [low_rest[SUB * i : SUB * (i + 1)] for i in range(n)]
    unit = [jnp.where(sub == j, 1.0, 0.0).astype(jnp.float32) for j in range(SUB)]
    upp = None
    weights = jnp.ones((SUB, TOP), jnp.float32)
    for b in range(n):
        first = SUB * b
        block, rest = rest[:SUB], rest[SUB:]
        low, low_rest = low_rest[:SUB], low_rest[SUB:]
        cols = [spread(block, first + j) for j in range(SUB)]
        weight, entry, a_line, low_line = [], [], [], []
        for k in range(SUB):
            weight.append(1.0 / line(cols[k], k))
            weights = jnp.where(lane == first + k, weight[k], weights)
            entry.append([line(cols[j], k) if j > k else None for j in range(SUB)])
            a_line.append(jnp.where(lane > first + k, line(block, k), 0.0))
            low_line.append(line(low, k))
            if k < SUB - 1:
                multiplier = jnp.where(sub > k, cols[k] * weight[k], 0.0)
                for j in range(k + 1, SUB):
                    cols[j] = cols[j] - multiplier * entry[k][j]
                block = block - multiplier * a_line[k]
                low = low - multiplier * low_line[k]
        lu_ref[first : first + SUB, :] = block
        linv_ref[first : first + SUB, :] = low

        def over(x, rows):
            return x[:1] if rows != SUB else x

        def multipliers(cols, rows):
            cols = list(cols)
            for k in range(SUB):
                cols[k] = cols[k] * over(weight[k], rows)
                for j in range(k + 1, SUB):
                    cols[j] = cols[j] - cols[k] * over(entry[k][j], rows)
            return cols

        rows = TOP - first - SUB
        if rows:
            part = multipliers([spread(rest, first + j) for j in range(SUB)], rows)
            for k in range(SUB):
                rest = rest - part[k] * over(a_line[k], rows)
                low_rest = low_rest - part[k] * over(low_line[k], rows)
        if upp is not None:
            part = multipliers([spread(upp, first + j) for j in range(SUB)], first)
            for k in range(SUB):
                upp = upp - part[k] * over(a_line[k], first)
        own = eye[b]
        part = multipliers(unit, SUB)
        for k in range(SUB):
            own = own - part[k] * a_line[k]
        upp = own if upp is None else jnp.concatenate([upp, own], axis=0)
    scale = weights[:1]
    packed = lu_ref[...]
    lu_ref[...] = jnp.where(row_id > lane_id, packed * scale, packed)
    uinv_ref[...] = upp * scale


def finish_kernel(
    pivot_ref,
    a_ref,
    panel_ref,
    leads_ref,
    news_ref,
    olds_ref,
    lu,
    linv,
    uinv,
    out_ref,
    a_buf,
    p_buf,
    news,
    olds,
    upper,
    solved,
    top_rows,
    in_sem,
    side_sem,
    out_sem,
):
    my_row = lax.axis_index("row")
    my_col = lax.axis_index("col")
    rows = a_buf.shape[0] // CHUNKS
    copies = [
        pltpu.make_async_copy(
            a_ref.at[pl.ds(rows * i, rows)], a_buf.at[pl.ds(rows * i, rows)], in_sem.at[i]
        )
        for i in range(CHUNKS)
    ]
    news_copy = pltpu.make_async_copy(news_ref, news, side_sem.at[0])
    olds_copy = pltpu.make_async_copy(olds_ref, olds, side_sem.at[1])
    panel_copy = pltpu.make_async_copy(panel_ref, p_buf, side_sem.at[2])
    for copy in (news_copy, olds_copy, panel_copy):
        copy.start()
    for copy in copies:
        copy.start()
    news_copy.wait()
    upper[...] = dot(linv[...], news[...].reshape(upper.shape))
    solved[...] = dot(uinv[...], upper[...])
    holds = my_col < 2
    own_lanes = (lax.broadcasted_iota(jnp.int32, (TOP, TOP), 1) < NB) & holds
    inverse = uinv[...]
    own = jnp.where(my_col == 0, inverse, pltpu.roll(inverse, NB, 1))
    solved[:, :TOP] = jnp.where(own_lanes, -own, solved[:, :TOP])
    top = pl.ds(pl.multiple_of(jnp.minimum(my_row, 1) * NB, NB), NB)
    corner = lu[top, :]
    corner = jnp.where(my_col == 0, corner, pltpu.roll(corner, NB, 1))
    top_rows[...] = upper[top, :]
    top_rows[:, :TOP] = jnp.where(own_lanes[:NB], corner, top_rows[:, :TOP])
    high, rest = halves(solved[...])
    twice = jnp.concatenate([high, high], axis=0)
    olds_copy.wait()
    panel_copy.wait()
    for copy in copies:
        copy.wait()

    chunk = olds.shape[1]
    bits = chunk.bit_length() - 1

    def place(step, carry):
        for j in range(PLACES):
            k = step * PLACES + j
            index = place_of(pivot_ref, k)

            @pl.when(index >= 0)
            def _():
                slot = k >> bits
                row = k & (chunk - 1)
                a_buf[pl.ds(index, 1), :] = olds[slot, pl.ds(row, 1), :]
                p_buf[pl.ds(index, 1), :] = leads_ref[slot, pl.ds(chunk + row, 1), :]

        return carry

    lax.fori_loop(0, TOP // PLACES, place, 0)
    dropped = (lax.broadcasted_iota(jnp.int32, (rows, a_buf.shape[1]), 1) < NB) & holds
    outs = []
    for i in range(CHUNKS):
        part = pl.ds(rows * i, rows)
        kept = jnp.where(dropped, 0.0, a_buf[part, :])
        left, left_rest = halves(p_buf[part, :])
        product = dot_pair(jnp.concatenate([left, left_rest], axis=1), twice)
        a_buf[part, :] = kept - (product + dot_pair(left, rest))
        if i == 0:

            @pl.when(my_row < 2)
            def _():
                a_buf[:NB, :] = top_rows[...]

        out = pltpu.make_async_copy(a_buf.at[part], out_ref.at[part], out_sem.at[i])
        out.start()
        outs.append(out)
    for out in outs:
        out.wait()


def finish(matrix, panel, leads, news, olds, lu, linv, uinv, pivots):
    any_spec = pl.BlockSpec(memory_space=pl.ANY)
    vmem = pl.BlockSpec(memory_space=pltpu.VMEM)
    return pl.pallas_call(
        finish_kernel,
        out_shape=jax.ShapeDtypeStruct(matrix.shape, jnp.float32),
        in_specs=[pl.BlockSpec(memory_space=pltpu.SMEM)]
        + [any_spec, any_spec, vmem, any_spec, any_spec, vmem, vmem, vmem],
        out_specs=any_spec,
        scratch_shapes=[
            pltpu.VMEM(matrix.shape, jnp.float32),
            pltpu.VMEM(panel.shape, jnp.float32),
            pltpu.VMEM(news.shape, jnp.float32),
            pltpu.VMEM(olds.shape, jnp.float32),
            pltpu.VMEM((TOP, matrix.shape[1]), jnp.float32),
            pltpu.VMEM((TOP, matrix.shape[1]), jnp.float32),
            pltpu.VMEM((NB, matrix.shape[1]), jnp.float32),
            pltpu.SemaphoreType.DMA((CHUNKS,)),
            pltpu.SemaphoreType.DMA((3,)),
            pltpu.SemaphoreType.DMA((CHUNKS,)),
        ],
        name="finish",
    )(pivots, matrix, panel, leads, news, olds, lu, linv, uinv)


def move_kernel(
    pivot_ref,
    a_ref,
    panel_ref,
    leads_ref,
    news_ref,
    olds_ref,
    lu_ref,
    linv_ref,
    uinv_ref,
    a_buf,
    lead_buf,
    picked_lead,
    pack,
    picked,
    parts,
    news,
    olds,
    tiles,
    tile_parts,
    tile_pair,
    leads,
    sums,
    panel,
    load_sem,
    slice_send,
    slice_recv,
    spread_send,
    pair_send,
    pair_recv,
    part_send,
    part_recv,
    top_send,
    top_recv,
    new_send,
    new_recv,
    old_send,
    old_recv,
    tile_send,
    tile_recv,
    fan_send,
    fan_recv,
    lead_send,
    lead_recv,
    panel_out,
    side_out,
):
    rows_dev = lax.axis_size("row")
    cols_dev = lax.axis_size("col")
    chips = cols_dev // 2
    my_row = lax.axis_index("row")
    my_col = lax.axis_index("col")
    chip = my_col // 2
    core = my_col % 2
    chunk = TOP // rows_dev
    half_rows = a_buf.shape[0] // 2
    slice_rows = half_rows // chips

    load_lead = pltpu.make_async_copy(a_ref.at[:, pl.ds(0, TOP)], lead_buf, load_sem.at[0])
    load = pltpu.make_async_copy(a_ref, a_buf, load_sem.at[1])

    @pl.when(chip == 0)
    def _():
        load_lead.start()

    load.start()
    barrier = pltpu.get_barrier_semaphore()
    for j in range(1, rows_dev):
        pl.semaphore_signal(
            barrier, inc=1, device_id={"row": lax.rem(my_row + j, rows_dev)}, device_id_type=MESH
        )
    for j in range(1, cols_dev):
        pl.semaphore_signal(
            barrier, inc=1, device_id={"col": lax.rem(my_col + j, cols_dev)}, device_id_type=MESH
        )

    def pick(table, target):
        def body(step, carry):
            for j in range(PLACES):
                k = step * PLACES + j
                index = place_of(pivot_ref, k)
                row = table[pl.ds(jnp.maximum(index, 0), 1), :]
                target[pl.ds(k, 1), :] = jnp.where(index >= 0, row, 0.0)
            return carry

        lax.fori_loop(0, TOP // PLACES, body, 0)

    first = lax.broadcasted_iota(jnp.int32, (slice_rows, TOP), 1) < NB
    first_tile = lax.broadcasted_iota(jnp.int32, (chunk, TOP), 1) < NB

    def top_start(d):
        return d * chunk - d * chunk // NB * NB

    @pl.when(chip == 0)
    def _():
        load_lead.wait()
        pick(lead_buf, picked_lead)
        for d in range(rows_dev):
            start = top_start(d)
            top = pltpu.roll(lead_buf[start : start + chunk, :], NB, 1)
            top = jnp.where(my_row == d * chunk // NB, top, 0.0)
            tiles[d] = jnp.where(first_tile, picked_lead[chunk * d : chunk * (d + 1), :], top)

    @pl.when(chip != 0)
    def _():
        load.wait()
        pick(a_buf, picked)

    pl.semaphore_wait(barrier, rows_dev + cols_dev - 2)

    def to_row(source, target, send, recv, d):
        return pltpu.make_async_remote_copy(
            src_ref=source,
            dst_ref=target,
            send_sem=send,
            recv_sem=recv,
            device_id={"row": d},
            device_id_type=MESH,
        )

    def to_col(source, target, send, recv, q):
        return pltpu.make_async_remote_copy(
            src_ref=source,
            dst_ref=target,
            send_sem=send,
            recv_sem=recv,
            device_id={"col": q},
            device_id_type=MESH,
        )

    def other(j):
        return lax.rem(my_row + j, rows_dev)

    def tile_copy(j):
        d = other(j)
        return to_row(
            tiles.at[d], tile_parts.at[my_row], tile_send.at[j], tile_recv.at[my_row], d
        )

    def slice_copy(s, t, send):
        return to_col(pack.at[core, s], pack.at[core, s], send, slice_recv.at[s], t * 2 + core)

    half = chunk // 2
    all_rows = pl.ds(0, chunk)

    def part_of(d, part=None):
        start, size = (0, chunk) if part is None else (part * half, half)
        return picked.at[pl.ds(d * chunk + start, size)]

    def part_copy(slot, target, relay, part=None):
        rows = all_rows if part is None else pl.ds(part * half, half)
        return to_row(
            part_of(other(target), part),
            parts.at[slot, rows],
            part_send.at[slot],
            part_recv.at[slot],
            other(relay),
        )

    def part_copies():
        return [
            part_copy(0, 7, 1),
            part_copy(1, 5, 7),
            part_copy(2, 4, 6, 0),
            part_copy(3, 1, 7),
            part_copy(4, 3, 1),
            part_copy(5, 4, 2, 1),
        ]

    def sum_copy(which, target):
        slot = 6 + which
        return to_row(
            sums.at[which], parts.at[slot], part_send.at[slot], part_recv.at[slot], other(target)
        )

    def value_of(d):
        return picked[pl.ds(pl.multiple_of(d * chunk, chunk), chunk), :]

    def top_copy(d):
        return to_row(
            a_buf.at[pl.ds(top_start(d), chunk), :], olds.at[d], top_send.at[d], top_recv, d
        )

    def ring_copy(j, table, send, recv):
        return to_row(table.at[my_row], table.at[my_row], send.at[j], recv.at[my_row], other(j))

    def arrive(j, table, send, recv):
        s = other(j)
        to_row(table.at[s], table.at[s], send.at[j], recv.at[s], s).wait_recv()

    def hop(table, slot, part, d, send, recv):
        return to_row(table.at[slot, part], table.at[slot, part], send, recv, d)

    def stage_one(table, send, recv):
        return [
            hop(table, my_row, all_rows, other(j), send.at[j], recv.at[my_row]) for j in (2, 6)
        ]

    def stage_two(table, send, recv):
        below, above = other(6), other(2)
        upper = pl.ds(0, half)
        lower = pl.ds(half, half)
        return [
            hop(table, below, all_rows, other(7), send.at[0], recv.at[below]),
            hop(table, below, all_rows, other(1), send.at[1], recv.at[below]),
            hop(table, below, upper, other(2), send.at[3], recv.at[below]),
            hop(table, above, all_rows, other(1), send.at[4], recv.at[above]),
            hop(table, above, all_rows, other(7), send.at[5], recv.at[above]),
            hop(table, above, lower, other(6), send.at[7], recv.at[rows_dev]),
        ]

    def begin(table, send, recv):
        for copy in stage_one(table, send, recv):
            copy.start()

    def forward(table, send, recv):
        arrive(6, table, send, recv)
        arrive(2, table, send, recv)
        for copy in stage_two(table, send, recv):
            copy.start()

    def gathered(table, send, recv):
        for j in (1, 3, 5, 7):
            arrive(j, table, send, recv)
        far = other(4)
        hop(table, far, pl.ds(0, half), far, send.at[0], recv.at[far]).wait_recv()
        hop(table, far, pl.ds(half, half), far, send.at[0], recv.at[rows_dev]).wait_recv()

    def sent(table, send, recv):
        for copy in stage_one(table, send, recv) + stage_two(table, send, recv):
            copy.wait_send()

    def fan_copy(j):
        q = lax.rem(my_col + j, cols_dev)
        return to_col(
            tile_pair.at[core], tile_pair.at[core], fan_send.at[j], fan_recv.at[core], q
        )

    @pl.when(chip == 0)
    def _():
        for j in range(1, rows_dev):
            tile_copy(j).start()
        tile_parts[my_row] = tiles[my_row]
        for s in range(chips):
            low = lead_buf[slice_rows * s : slice_rows * (s + 1), :]
            high = lead_buf[half_rows + slice_rows * s : half_rows + slice_rows * (s + 1), :]
            at_zero = jnp.where(core == 0, low, high)
            shifted = jnp.where(core == 0, high, low)
            pack[core, s] = jnp.where(first, at_zero, pltpu.roll(shifted, NB, 1))
        for s in range(1, chips):
            slice_copy(s, s, slice_send.at[s]).start()
        load.wait()
        pick(a_buf, picked)

    for copy in part_copies():
        copy.start()
    for d in range(rows_dev):
        owner = d * chunk // NB

        @pl.when(my_row == owner)
        def _():
            if d == owner:
                olds[d] = a_buf[top_start(d) : top_start(d) + chunk, :]
            else:
                top_copy(d).start()

    @pl.when(chip == 0)
    def _():
        for j in range(1, rows_dev):
            arrive(j, tile_parts, tile_send, tile_recv)
        total = tile_parts[0]
        for s in range(1, rows_dev):
            total = total + tile_parts[s]
        tile_pair[core] = total
        for j in range(1, cols_dev):
            fan_copy(j).start()

    @pl.when(chip != 0)
    def _():
        slice_copy(chip, chip, slice_send.at[0]).wait_recv()

    for j in range(1, chips):
        t = lax.rem(chip + j, chips)

        @pl.when(t != 0)
        def _():
            slice_copy(chip, t, spread_send.at[j]).start()

    for d in range(rows_dev):
        if d != d * chunk // NB:

            @pl.when(my_row == d)
            def _():
                top_copy(d).wait_recv()

    begin(olds, old_send, old_recv)
    for copy in part_copies():
        copy.wait_recv()
    low_sum = value_of(other(6)) + parts[0] + parts[1]
    sums[0, :half] = low_sum[:half] + parts[2, :half]
    sums[0, half:] = low_sum[half:]
    high_sum = value_of(other(2)) + parts[3] + parts[4]
    sums[1, :half] = high_sum[:half]
    sums[1, half:] = high_sum[half:] + parts[5, half:]
    sum_copy(0, 6).start()
    sum_copy(1, 2).start()
    forward(olds, old_send, old_recv)
    sum_copy(0, 6).wait_recv()
    sum_copy(1, 2).wait_recv()
    news[my_row] = value_of(my_row) + parts[6] + parts[7]
    begin(news, new_send, new_recv)

    for c in range(2):

        @pl.when(my_col != c)
        def _():
            to_col(
                tile_pair.at[c], tile_pair.at[c], fan_send.at[0], fan_recv.at[c], c
            ).wait_recv()

    zero_tile = tile_pair[0]
    one_tile = tile_pair[1]
    leads[my_row, :chunk] = jnp.where(first_tile, zero_tile, pltpu.roll(one_tile, NB, 1))
    leads[my_row, chunk:] = jnp.where(first_tile, pltpu.roll(zero_tile, NB, 1), one_tile)
    for j in range(1, rows_dev):
        ring_copy(j, leads, lead_send, lead_recv).start()
    forward(news, new_send, new_recv)

    groups = min(4, chips)
    per = chips // groups

    def panel_copies(g):
        size = per * slice_rows
        copies = []
        for side in range(2):
            rows = pl.ds(side * half_rows + g * size, size)
            copies.append(
                pltpu.make_async_copy(panel.at[rows], panel_ref.at[rows], panel_out.at[2 * g + side])
            )
        return copies

    def pair_copy(g, which):
        held = pack.at[which, pl.ds(g * per, per)]
        return to_col(held, held, pair_send.at[g], pair_recv.at[g], chip * 2 + 1 - core)

    for g in range(groups):

        @pl.when(chip != 0)
        def _():
            for s in range(g * per, (g + 1) * per):

                @pl.when(chip != s)
                def _():
                    slice_copy(s, chip, slice_send.at[0]).wait_recv()

        pair_copy(g, core).start()

    for j in range(1, rows_dev):
        arrive(j, leads, lead_send, lead_recv)
    factor(leads, lu_ref, linv_ref, uinv_ref)

    for g in range(groups):
        pair_copy(g, 1 - core).wait_recv()
        for s in range(g * per, (g + 1) * per):
            zero_pack = pack[0, s]
            one_pack = pack[1, s]
            low = slice(slice_rows * s, slice_rows * (s + 1))
            high = slice(half_rows + slice_rows * s, half_rows + slice_rows * (s + 1))
            panel[low, :] = jnp.where(first, zero_pack, one_pack)
            panel[high, :] = pltpu.roll(jnp.where(first, one_pack, zero_pack), NB, 1)
        for copy in panel_copies(g):
            copy.start()

    side = [
        pltpu.make_async_copy(table, target, side_out.at[i])
        for i, (table, target) in enumerate(
            ((leads, leads_ref), (news, news_ref), (olds, olds_ref))
        )
    ]
    side[0].start()
    gathered(olds, old_send, old_recv)
    side[2].start()
    gathered(news, new_send, new_recv)
    side[1].start()

    for copy in part_copies():
        copy.wait_send()
    sum_copy(0, 6).wait_send()
    sum_copy(1, 2).wait_send()
    for j in range(1, rows_dev):
        ring_copy(j, leads, lead_send, lead_recv).wait_send()
    sent(news, new_send, new_recv)
    sent(olds, old_send, old_recv)
    for d in range(rows_dev):
        owner = d * chunk // NB
        if d != owner:

            @pl.when(my_row == owner)
            def _():
                top_copy(d).wait_send()

    @pl.when(chip == 0)
    def _():
        for j in range(1, rows_dev):
            tile_copy(j).wait_send()
        for s in range(1, chips):
            slice_copy(s, s, slice_send.at[s]).wait_send()
        for j in range(1, cols_dev):
            fan_copy(j).wait_send()

    for j in range(1, chips):
        t = lax.rem(chip + j, chips)

        @pl.when(t != 0)
        def _():
            slice_copy(chip, t, spread_send.at[j]).wait_send()

    for g in range(groups):
        pair_copy(g, core).wait_send()
        for copy in panel_copies(g):
            copy.wait()
    for copy in side:
        copy.wait()


def move(matrix, pivots):
    rows_dev = lax.axis_size("row")
    cols_dev = lax.axis_size("col")
    chips = cols_dev // 2
    chunk = TOP // rows_dev
    rows, cols = matrix.shape
    dma = pltpu.SemaphoreType.DMA
    f32 = jnp.float32
    by_row = dma((rows_dev,))
    by_chip = dma((chips,))
    return pl.pallas_call(
        move_kernel,
        out_shape=[
            jax.ShapeDtypeStruct((rows, TOP), f32),
            jax.ShapeDtypeStruct((rows_dev, 2 * chunk, TOP), f32),
            jax.ShapeDtypeStruct((rows_dev, chunk, cols), f32),
            jax.ShapeDtypeStruct((rows_dev, chunk, cols), f32),
            *[jax.ShapeDtypeStruct((TOP, TOP), f32)] * 3,
        ],
        in_specs=[
            pl.BlockSpec(memory_space=pltpu.SMEM),
            pl.BlockSpec(memory_space=pl.ANY),
        ],
        out_specs=[pl.BlockSpec(memory_space=pl.ANY)] * 4
        + [pl.BlockSpec(memory_space=pltpu.VMEM)] * 3,
        scratch_shapes=[
            pltpu.VMEM((rows, cols), f32),
            pltpu.VMEM((rows, TOP), f32),
            pltpu.VMEM((TOP, TOP), f32),
            pltpu.VMEM((2, chips, rows // 2 // chips, TOP), f32),
            pltpu.VMEM((TOP, cols), f32),
            pltpu.VMEM((rows_dev, chunk, cols), f32),
            pltpu.VMEM((rows_dev, chunk, cols), f32),
            pltpu.VMEM((rows_dev, chunk, cols), f32),
            pltpu.VMEM((rows_dev, chunk, TOP), f32),
            pltpu.VMEM((rows_dev, chunk, TOP), f32),
            pltpu.VMEM((2, chunk, TOP), f32),
            pltpu.VMEM((rows_dev, 2 * chunk, TOP), f32),
            pltpu.VMEM((2, chunk, cols), f32),
            pltpu.VMEM((rows, TOP), f32),
            dma((2,)),
            by_chip,
            by_chip,
            by_chip,
            dma((4,)),
            dma((4,)),
            by_row,
            by_row,
            by_row,
            dma,
            by_row,
            dma((rows_dev + 1,)),
            by_row,
            dma((rows_dev + 1,)),
            by_row,
            by_row,
            dma((cols_dev,)),
            dma((2,)),
            by_row,
            by_row,
            dma((8,)),
            dma((3,)),
        ],
        compiler_params=pltpu.CompilerParams(collective_id=0, has_side_effects=True),
        name="move",
    )(pivots, matrix)


def shards(matrix, pivots):
    panel, leads, news, olds, lu, linv, uinv = move(matrix, pivots)
    return finish(matrix, panel, leads, news, olds, lu, linv, uinv, pivots)


def solution(mesh):
    placed = (P("row", "col"), P())
    return jax.shard_map(
        shards, mesh=mesh, in_specs=placed, out_specs=P("row", "col"), check_vma=False
    )
```

```python
import jax
import jax.numpy as jnp
from jax import lax
from jax.experimental import pallas as pl
from jax.experimental.pallas import tpu as pltpu
from jax.sharding import PartitionSpec as P

NB = 64
TOP = 2 * NB
SUB = 8
CHUNKS = 8
PLACES = 8
MESH = pl.DeviceIdType.MESH


def place_of(pivot_ref, k):
    grid_rows = lax.axis_size("row")
    bits = NB.bit_length() - 1
    pivot = pivot_ref[k >> bits, k & (NB - 1)]
    local = (pivot >> (bits + grid_rows.bit_length() - 1) << bits) + (pivot & (NB - 1))
    mine = (pivot >> bits & (grid_rows - 1)) == lax.axis_index("row")
    return jnp.where(mine, local, -1)


def halves(x):
    high = x.astype(jnp.bfloat16)
    return high, (x - high.astype(jnp.float32)).astype(jnp.bfloat16)


def dot_pair(a, b):
    return lax.dot_general(
        a, b, (((1,), (0,)), ((), ())), preferred_element_type=jnp.float32
    )


def dot(a, b):
    high, rest = halves(a)
    b_high, b_rest = halves(b)
    both = jnp.concatenate([high, rest], axis=1)
    return dot_pair(both, jnp.concatenate([b_high, b_high], axis=0)) + dot_pair(high, b_rest)


def spread(block, lane):
    return jnp.broadcast_to(block[:, lane : lane + 1], block.shape)


def line(block, row):
    return jnp.broadcast_to(block[row : row + 1, :], block.shape)


def factor(a_ref, lu_ref, linv_ref, uinv_ref):
    n = TOP // SUB
    chunk = a_ref.shape[1] // 2
    lane = lax.broadcasted_iota(jnp.int32, (SUB, TOP), 1)
    sub = lax.broadcasted_iota(jnp.int32, (SUB, TOP), 0)
    row_id = lax.broadcasted_iota(jnp.int32, (TOP, TOP), 0)
    lane_id = lax.broadcasted_iota(jnp.int32, (TOP, TOP), 1)
    rest = jnp.concatenate([a_ref[slot, :chunk] for slot in range(TOP // chunk)], axis=0)
    low_rest = jnp.where(row_id == lane_id, 1.0, 0.0).astype(jnp.float32)
    eye = [low_rest[SUB * i : SUB * (i + 1)] for i in range(n)]
    unit = [jnp.where(sub == j, 1.0, 0.0).astype(jnp.float32) for j in range(SUB)]
    upp = None
    weights = jnp.ones((SUB, TOP), jnp.float32)
    for b in range(n):
        first = SUB * b
        block, rest = rest[:SUB], rest[SUB:]
        low, low_rest = low_rest[:SUB], low_rest[SUB:]
        cols = [spread(block, first + j) for j in range(SUB)]
        weight, entry, a_line, low_line = [], [], [], []
        for k in range(SUB):
            weight.append(1.0 / line(cols[k], k))
            weights = jnp.where(lane == first + k, weight[k], weights)
            entry.append([line(cols[j], k) if j > k else None for j in range(SUB)])
            a_line.append(jnp.where(lane > first + k, line(block, k), 0.0))
            low_line.append(line(low, k))
            if k < SUB - 1:
                multiplier = jnp.where(sub > k, cols[k] * weight[k], 0.0)
                for j in range(k + 1, SUB):
                    cols[j] = cols[j] - multiplier * entry[k][j]
                block = block - multiplier * a_line[k]
                low = low - multiplier * low_line[k]
        lu_ref[first : first + SUB, :] = block
        linv_ref[first : first + SUB, :] = low

        def over(x, rows):
            return x[:1] if rows != SUB else x

        def multipliers(cols, rows):
            cols = list(cols)
            for k in range(SUB):
                cols[k] = cols[k] * over(weight[k], rows)
                for j in range(k + 1, SUB):
                    cols[j] = cols[j] - cols[k] * over(entry[k][j], rows)
            return cols

        rows = TOP - first - SUB
        if rows:
            part = multipliers([spread(rest, first + j) for j in range(SUB)], rows)
            for k in range(SUB):
                rest = rest - part[k] * over(a_line[k], rows)
                low_rest = low_rest - part[k] * over(low_line[k], rows)
        if upp is not None:
            part = multipliers([spread(upp, first + j) for j in range(SUB)], first)
            for k in range(SUB):
                upp = upp - part[k] * over(a_line[k], first)
        own = eye[b]
        part = multipliers(unit, SUB)
        for k in range(SUB):
            own = own - part[k] * a_line[k]
        upp = own if upp is None else jnp.concatenate([upp, own], axis=0)
    scale = weights[:1]
    packed = lu_ref[...]
    lu_ref[...] = jnp.where(row_id > lane_id, packed * scale, packed)
    uinv_ref[...] = upp * scale


def finish_kernel(
    pivot_ref,
    a_ref,
    panel_ref,
    leads_ref,
    news_ref,
    olds_ref,
    lu,
    linv,
    uinv,
    out_ref,
    a_buf,
    p_buf,
    news,
    olds,
    upper,
    solved,
    top_rows,
    in_sem,
    side_sem,
    out_sem,
):
    my_row = lax.axis_index("row")
    my_col = lax.axis_index("col")
    spare = a_buf.shape[0] - SUB
    rows = spare // CHUNKS
    copies = [
        pltpu.make_async_copy(
            a_ref.at[pl.ds(rows * i, rows)], a_buf.at[pl.ds(rows * i, rows)], in_sem.at[i]
        )
        for i in range(CHUNKS)
    ]
    news_copy = pltpu.make_async_copy(news_ref, news, side_sem.at[0])
    olds_copy = pltpu.make_async_copy(olds_ref, olds, side_sem.at[1])
    panel_copy = pltpu.make_async_copy(panel_ref, p_buf.at[pl.ds(0, spare)], side_sem.at[2])
    for copy in (news_copy, olds_copy, panel_copy):
        copy.start()
    for copy in copies:
        copy.start()
    news_copy.wait()
    upper[...] = dot(linv[...], news[...].reshape(upper.shape))
    solved[...] = dot(uinv[...], upper[...])
    holds = my_col < 2
    own_lanes = (lax.broadcasted_iota(jnp.int32, (TOP, TOP), 1) < NB) & holds
    inverse = uinv[...]
    own = jnp.where(my_col == 0, inverse, pltpu.roll(inverse, NB, 1))
    solved[:, :TOP] = jnp.where(own_lanes, -own, solved[:, :TOP])
    top = pl.ds(pl.multiple_of(jnp.minimum(my_row, 1) * NB, NB), NB)
    corner = lu[top, :]
    corner = jnp.where(my_col == 0, corner, pltpu.roll(corner, NB, 1))
    top_rows[...] = upper[top, :]
    top_rows[:, :TOP] = jnp.where(own_lanes[:NB], corner, top_rows[:, :TOP])
    high, rest = halves(solved[...])
    twice = jnp.concatenate([high, high], axis=0)
    olds_copy.wait()
    panel_copy.wait()
    for copy in copies:
        copy.wait()

    chunk = olds.shape[1]

    def place(slot, carry):
        for row in range(chunk):
            index = place_of(pivot_ref, slot * chunk + row)
            index = jnp.where(index < 0, spare, index)
            a_buf[pl.ds(index, 1), :] = olds[slot, row : row + 1, :]
            p_buf[pl.ds(index, 1), :] = leads_ref[slot, chunk + row : chunk + row + 1, :]
        return carry

    lax.fori_loop(0, TOP // chunk, place, 0)
    dropped = (lax.broadcasted_iota(jnp.int32, (rows, a_buf.shape[1]), 1) < NB) & holds
    outs = []
    for i in range(CHUNKS):
        part = pl.ds(rows * i, rows)
        kept = jnp.where(dropped, 0.0, a_buf[part, :])
        left, left_rest = halves(p_buf[part, :])
        product = dot_pair(jnp.concatenate([left, left_rest], axis=1), twice)
        a_buf[part, :] = kept - (product + dot_pair(left, rest))
        if i == 0:

            @pl.when(my_row < 2)
            def _():
                a_buf[:NB, :] = top_rows[...]

        out = pltpu.make_async_copy(a_buf.at[part], out_ref.at[part], out_sem.at[i])
        out.start()
        outs.append(out)
    for out in outs:
        out.wait()


def finish(matrix, panel, leads, news, olds, lu, linv, uinv, pivots):
    any_spec = pl.BlockSpec(memory_space=pl.ANY)
    vmem = pl.BlockSpec(memory_space=pltpu.VMEM)
    return pl.pallas_call(
        finish_kernel,
        out_shape=jax.ShapeDtypeStruct(matrix.shape, jnp.float32),
        in_specs=[pl.BlockSpec(memory_space=pltpu.SMEM)]
        + [any_spec, any_spec, vmem, any_spec, any_spec, vmem, vmem, vmem],
        out_specs=any_spec,
        scratch_shapes=[
            pltpu.VMEM((matrix.shape[0] + SUB, matrix.shape[1]), jnp.float32),
            pltpu.VMEM((panel.shape[0] + SUB, TOP), jnp.float32),
            pltpu.VMEM(news.shape, jnp.float32),
            pltpu.VMEM(olds.shape, jnp.float32),
            pltpu.VMEM((TOP, matrix.shape[1]), jnp.float32),
            pltpu.VMEM((TOP, matrix.shape[1]), jnp.float32),
            pltpu.VMEM((NB, matrix.shape[1]), jnp.float32),
            pltpu.SemaphoreType.DMA((CHUNKS,)),
            pltpu.SemaphoreType.DMA((3,)),
            pltpu.SemaphoreType.DMA((CHUNKS,)),
        ],
        name="finish",
    )(pivots, matrix, panel, leads, news, olds, lu, linv, uinv)


def move_kernel(
    pivot_ref,
    a_ref,
    panel_ref,
    leads_ref,
    news_ref,
    olds_ref,
    lu_ref,
    linv_ref,
    uinv_ref,
    a_buf,
    lead_buf,
    picked_lead,
    pack,
    picked,
    parts,
    news,
    olds,
    tiles,
    tile_parts,
    tile_pair,
    leads,
    sums,
    panel,
    load_sem,
    slice_send,
    slice_recv,
    spread_send,
    pair_send,
    pair_recv,
    part_send,
    part_recv,
    top_send,
    top_recv,
    new_send,
    new_recv,
    old_send,
    old_recv,
    tile_send,
    tile_recv,
    fan_send,
    fan_recv,
    lead_send,
    lead_recv,
    panel_out,
    side_out,
):
    rows_dev = lax.axis_size("row")
    cols_dev = lax.axis_size("col")
    chips = cols_dev // 2
    my_row = lax.axis_index("row")
    my_col = lax.axis_index("col")
    chip = my_col // 2
    core = my_col % 2
    chunk = TOP // rows_dev
    half_rows = a_buf.shape[0] // 2
    slice_rows = half_rows // chips

    load_lead = pltpu.make_async_copy(a_ref.at[:, pl.ds(0, TOP)], lead_buf, load_sem.at[0])
    load = pltpu.make_async_copy(a_ref, a_buf, load_sem.at[1])

    @pl.when(chip == 0)
    def _():
        load_lead.start()

    load.start()
    barrier = pltpu.get_barrier_semaphore()
    for j in range(1, rows_dev):
        pl.semaphore_signal(
            barrier, inc=1, device_id={"row": lax.rem(my_row + j, rows_dev)}, device_id_type=MESH
        )
    for j in range(1, cols_dev):
        pl.semaphore_signal(
            barrier, inc=1, device_id={"col": lax.rem(my_col + j, cols_dev)}, device_id_type=MESH
        )

    def pick(table, target):
        def body(step, carry):
            for j in range(PLACES):
                k = step * PLACES + j
                index = place_of(pivot_ref, k)
                row = table[pl.ds(jnp.maximum(index, 0), 1), :]
                target[pl.ds(k, 1), :] = jnp.where(index >= 0, row, 0.0)
            return carry

        lax.fori_loop(0, TOP // PLACES, body, 0)

    first = lax.broadcasted_iota(jnp.int32, (slice_rows, TOP), 1) < NB
    first_tile = lax.broadcasted_iota(jnp.int32, (chunk, TOP), 1) < NB

    def top_start(d):
        return d * chunk - d * chunk // NB * NB

    @pl.when(chip == 0)
    def _():
        load_lead.wait()
        pick(lead_buf, picked_lead)
        for d in range(rows_dev):
            start = top_start(d)
            top = pltpu.roll(lead_buf[start : start + chunk, :], NB, 1)
            top = jnp.where(my_row == d * chunk // NB, top, 0.0)
            tiles[d] = jnp.where(first_tile, picked_lead[chunk * d : chunk * (d + 1), :], top)

    @pl.when(chip != 0)
    def _():
        load.wait()
        pick(a_buf, picked)

    pl.semaphore_wait(barrier, rows_dev + cols_dev - 2)

    def to_row(source, target, send, recv, d):
        return pltpu.make_async_remote_copy(
            src_ref=source,
            dst_ref=target,
            send_sem=send,
            recv_sem=recv,
            device_id={"row": d},
            device_id_type=MESH,
        )

    def to_col(source, target, send, recv, q):
        return pltpu.make_async_remote_copy(
            src_ref=source,
            dst_ref=target,
            send_sem=send,
            recv_sem=recv,
            device_id={"col": q},
            device_id_type=MESH,
        )

    def other(j):
        return lax.rem(my_row + j, rows_dev)

    def tile_copy(j):
        d = other(j)
        return to_row(
            tiles.at[d], tile_parts.at[my_row], tile_send.at[j], tile_recv.at[my_row], d
        )

    def slice_copy(s, t, send):
        return to_col(pack.at[core, s], pack.at[core, s], send, slice_recv.at[s], t * 2 + core)

    half = chunk // 2
    all_rows = pl.ds(0, chunk)

    def part_of(d, part=None):
        start, size = (0, chunk) if part is None else (part * half, half)
        return picked.at[pl.ds(d * chunk + start, size)]

    def part_copy(slot, target, relay, part=None):
        rows = all_rows if part is None else pl.ds(part * half, half)
        return to_row(
            part_of(other(target), part),
            parts.at[slot, rows],
            part_send.at[slot],
            part_recv.at[slot],
            other(relay),
        )

    def part_copies():
        return [
            part_copy(0, 7, 1),
            part_copy(1, 5, 7),
            part_copy(2, 4, 6, 0),
            part_copy(3, 1, 7),
            part_copy(4, 3, 1),
            part_copy(5, 4, 2, 1),
        ]

    def sum_copy(which, target):
        slot = 6 + which
        return to_row(
            sums.at[which], parts.at[slot], part_send.at[slot], part_recv.at[slot], other(target)
        )

    def value_of(d):
        return picked[pl.ds(pl.multiple_of(d * chunk, chunk), chunk), :]

    def top_copy(d):
        return to_row(
            a_buf.at[pl.ds(top_start(d), chunk), :], olds.at[d], top_send.at[d], top_recv, d
        )

    def ring_copy(j, table, send, recv):
        return to_row(table.at[my_row], table.at[my_row], send.at[j], recv.at[my_row], other(j))

    def arrive(j, table, send, recv):
        s = other(j)
        to_row(table.at[s], table.at[s], send.at[j], recv.at[s], s).wait_recv()

    def hop(table, slot, part, d, send, recv):
        return to_row(table.at[slot, part], table.at[slot, part], send, recv, d)

    def stage_one(table, send, recv):
        return [
            hop(table, my_row, all_rows, other(j), send.at[j], recv.at[my_row]) for j in (2, 6)
        ]

    def stage_two(table, send, recv):
        below, above = other(6), other(2)
        upper = pl.ds(0, half)
        lower = pl.ds(half, half)
        return [
            hop(table, below, all_rows, other(7), send.at[0], recv.at[below]),
            hop(table, below, all_rows, other(1), send.at[1], recv.at[below]),
            hop(table, below, upper, other(2), send.at[3], recv.at[below]),
            hop(table, above, all_rows, other(1), send.at[4], recv.at[above]),
            hop(table, above, all_rows, other(7), send.at[5], recv.at[above]),
            hop(table, above, lower, other(6), send.at[7], recv.at[rows_dev]),
        ]

    def begin(table, send, recv):
        for copy in stage_one(table, send, recv):
            copy.start()

    def forward(table, send, recv):
        arrive(6, table, send, recv)
        arrive(2, table, send, recv)
        for copy in stage_two(table, send, recv):
            copy.start()

    def gathered(table, send, recv):
        for j in (1, 3, 5, 7):
            arrive(j, table, send, recv)
        far = other(4)
        hop(table, far, pl.ds(0, half), far, send.at[0], recv.at[far]).wait_recv()
        hop(table, far, pl.ds(half, half), far, send.at[0], recv.at[rows_dev]).wait_recv()

    def sent(table, send, recv):
        for copy in stage_one(table, send, recv) + stage_two(table, send, recv):
            copy.wait_send()

    def fan_copy(j):
        q = lax.rem(my_col + j, cols_dev)
        return to_col(
            tile_pair.at[core], tile_pair.at[core], fan_send.at[j], fan_recv.at[core], q
        )

    @pl.when(chip == 0)
    def _():
        for j in range(1, rows_dev):
            tile_copy(j).start()
        tile_parts[my_row] = tiles[my_row]
        for s in range(chips):
            low = lead_buf[slice_rows * s : slice_rows * (s + 1), :]
            high = lead_buf[half_rows + slice_rows * s : half_rows + slice_rows * (s + 1), :]
            at_zero = jnp.where(core == 0, low, high)
            shifted = jnp.where(core == 0, high, low)
            pack[core, s] = jnp.where(first, at_zero, pltpu.roll(shifted, NB, 1))
        for s in range(1, chips):
            slice_copy(s, s, slice_send.at[s]).start()
        load.wait()
        pick(a_buf, picked)

    for copy in part_copies():
        copy.start()
    for d in range(rows_dev):
        owner = d * chunk // NB

        @pl.when(my_row == owner)
        def _():
            if d == owner:
                olds[d] = a_buf[top_start(d) : top_start(d) + chunk, :]
            else:
                top_copy(d).start()

    @pl.when(chip == 0)
    def _():
        for j in range(1, rows_dev):
            arrive(j, tile_parts, tile_send, tile_recv)
        total = tile_parts[0]
        for s in range(1, rows_dev):
            total = total + tile_parts[s]
        tile_pair[core] = total
        for j in range(1, cols_dev):
            fan_copy(j).start()

    @pl.when(chip != 0)
    def _():
        slice_copy(chip, chip, slice_send.at[0]).wait_recv()

    for j in range(1, chips):
        t = lax.rem(chip + j, chips)

        @pl.when(t != 0)
        def _():
            slice_copy(chip, t, spread_send.at[j]).start()

    for d in range(rows_dev):
        if d != d * chunk // NB:

            @pl.when(my_row == d)
            def _():
                top_copy(d).wait_recv()

    begin(olds, old_send, old_recv)
    for copy in part_copies():
        copy.wait_recv()
    low_sum = value_of(other(6)) + parts[0] + parts[1]
    sums[0, :half] = low_sum[:half] + parts[2, :half]
    sums[0, half:] = low_sum[half:]
    high_sum = value_of(other(2)) + parts[3] + parts[4]
    sums[1, :half] = high_sum[:half]
    sums[1, half:] = high_sum[half:] + parts[5, half:]
    sum_copy(0, 6).start()
    sum_copy(1, 2).start()
    forward(olds, old_send, old_recv)
    sum_copy(0, 6).wait_recv()
    sum_copy(1, 2).wait_recv()
    news[my_row] = value_of(my_row) + parts[6] + parts[7]
    begin(news, new_send, new_recv)

    for c in range(2):

        @pl.when(my_col != c)
        def _():
            to_col(
                tile_pair.at[c], tile_pair.at[c], fan_send.at[0], fan_recv.at[c], c
            ).wait_recv()

    zero_tile = tile_pair[0]
    one_tile = tile_pair[1]
    leads[my_row, :chunk] = jnp.where(first_tile, zero_tile, pltpu.roll(one_tile, NB, 1))
    leads[my_row, chunk:] = jnp.where(first_tile, pltpu.roll(zero_tile, NB, 1), one_tile)
    for j in range(1, rows_dev):
        ring_copy(j, leads, lead_send, lead_recv).start()
    forward(news, new_send, new_recv)

    groups = min(4, chips)
    per = chips // groups

    def panel_copies(g):
        size = per * slice_rows
        copies = []
        for side in range(2):
            rows = pl.ds(side * half_rows + g * size, size)
            copies.append(
                pltpu.make_async_copy(panel.at[rows], panel_ref.at[rows], panel_out.at[2 * g + side])
            )
        return copies

    def pair_copy(g, which):
        held = pack.at[which, pl.ds(g * per, per)]
        return to_col(held, held, pair_send.at[g], pair_recv.at[g], chip * 2 + 1 - core)

    for g in range(groups):

        @pl.when(chip != 0)
        def _():
            for s in range(g * per, (g + 1) * per):

                @pl.when(chip != s)
                def _():
                    slice_copy(s, chip, slice_send.at[0]).wait_recv()

        pair_copy(g, core).start()

    for j in range(1, rows_dev):
        arrive(j, leads, lead_send, lead_recv)
    factor(leads, lu_ref, linv_ref, uinv_ref)

    for g in range(groups):
        pair_copy(g, 1 - core).wait_recv()
        for s in range(g * per, (g + 1) * per):
            zero_pack = pack[0, s]
            one_pack = pack[1, s]
            low = slice(slice_rows * s, slice_rows * (s + 1))
            high = slice(half_rows + slice_rows * s, half_rows + slice_rows * (s + 1))
            panel[low, :] = jnp.where(first, zero_pack, one_pack)
            panel[high, :] = pltpu.roll(jnp.where(first, one_pack, zero_pack), NB, 1)
        for copy in panel_copies(g):
            copy.start()

    side = [
        pltpu.make_async_copy(table, target, side_out.at[i])
        for i, (table, target) in enumerate(
            ((leads, leads_ref), (news, news_ref), (olds, olds_ref))
        )
    ]
    side[0].start()
    gathered(olds, old_send, old_recv)
    side[2].start()
    gathered(news, new_send, new_recv)
    side[1].start()

    for copy in part_copies():
        copy.wait_send()
    sum_copy(0, 6).wait_send()
    sum_copy(1, 2).wait_send()
    for j in range(1, rows_dev):
        ring_copy(j, leads, lead_send, lead_recv).wait_send()
    sent(news, new_send, new_recv)
    sent(olds, old_send, old_recv)
    for d in range(rows_dev):
        owner = d * chunk // NB
        if d != owner:

            @pl.when(my_row == owner)
            def _():
                top_copy(d).wait_send()

    @pl.when(chip == 0)
    def _():
        for j in range(1, rows_dev):
            tile_copy(j).wait_send()
        for s in range(1, chips):
            slice_copy(s, s, slice_send.at[s]).wait_send()
        for j in range(1, cols_dev):
            fan_copy(j).wait_send()

    for j in range(1, chips):
        t = lax.rem(chip + j, chips)

        @pl.when(t != 0)
        def _():
            slice_copy(chip, t, spread_send.at[j]).wait_send()

    for g in range(groups):
        pair_copy(g, core).wait_send()
        for copy in panel_copies(g):
            copy.wait()
    for copy in side:
        copy.wait()


def move(matrix, pivots):
    rows_dev = lax.axis_size("row")
    cols_dev = lax.axis_size("col")
    chips = cols_dev // 2
    chunk = TOP // rows_dev
    rows, cols = matrix.shape
    dma = pltpu.SemaphoreType.DMA
    f32 = jnp.float32
    by_row = dma((rows_dev,))
    by_chip = dma((chips,))
    return pl.pallas_call(
        move_kernel,
        out_shape=[
            jax.ShapeDtypeStruct((rows, TOP), f32),
            jax.ShapeDtypeStruct((rows_dev, 2 * chunk, TOP), f32),
            jax.ShapeDtypeStruct((rows_dev, chunk, cols), f32),
            jax.ShapeDtypeStruct((rows_dev, chunk, cols), f32),
            *[jax.ShapeDtypeStruct((TOP, TOP), f32)] * 3,
        ],
        in_specs=[
            pl.BlockSpec(memory_space=pltpu.SMEM),
            pl.BlockSpec(memory_space=pl.ANY),
        ],
        out_specs=[pl.BlockSpec(memory_space=pl.ANY)] * 4
        + [pl.BlockSpec(memory_space=pltpu.VMEM)] * 3,
        scratch_shapes=[
            pltpu.VMEM((rows, cols), f32),
            pltpu.VMEM((rows, TOP), f32),
            pltpu.VMEM((TOP, TOP), f32),
            pltpu.VMEM((2, chips, rows // 2 // chips, TOP), f32),
            pltpu.VMEM((TOP, cols), f32),
            pltpu.VMEM((rows_dev, chunk, cols), f32),
            pltpu.VMEM((rows_dev, chunk, cols), f32),
            pltpu.VMEM((rows_dev, chunk, cols), f32),
            pltpu.VMEM((rows_dev, chunk, TOP), f32),
            pltpu.VMEM((rows_dev, chunk, TOP), f32),
            pltpu.VMEM((2, chunk, TOP), f32),
            pltpu.VMEM((rows_dev, 2 * chunk, TOP), f32),
            pltpu.VMEM((2, chunk, cols), f32),
            pltpu.VMEM((rows, TOP), f32),
            dma((2,)),
            by_chip,
            by_chip,
            by_chip,
            dma((4,)),
            dma((4,)),
            by_row,
            by_row,
            by_row,
            dma,
            by_row,
            dma((rows_dev + 1,)),
            by_row,
            dma((rows_dev + 1,)),
            by_row,
            by_row,
            dma((cols_dev,)),
            dma((2,)),
            by_row,
            by_row,
            dma((8,)),
            dma((3,)),
        ],
        compiler_params=pltpu.CompilerParams(collective_id=0, has_side_effects=True),
        name="move",
    )(pivots, matrix)


def shards(matrix, pivots):
    panel, leads, news, olds, lu, linv, uinv = move(matrix, pivots)
    return finish(matrix, panel, leads, news, olds, lu, linv, uinv, pivots)


def solution(mesh):
    placed = (P("row", "col"), P())
    return jax.shard_map(
        shards, mesh=mesh, in_specs=placed, out_specs=P("row", "col"), check_vma=False
    )
```

```python
import jax
import jax.numpy as jnp
from jax import lax
from jax.experimental import pallas as pl
from jax.experimental.pallas import tpu as pltpu
from jax.sharding import PartitionSpec as P

NB = 64
TOP = 2 * NB
SUB = 8
CHUNKS = 8
PLACES = 8
MESH = pl.DeviceIdType.MESH


def place_of(pivot_ref, k):
    grid_rows = lax.axis_size("row")
    bits = NB.bit_length() - 1
    pivot = pivot_ref[k >> bits, k & (NB - 1)]
    local = (pivot >> (bits + grid_rows.bit_length() - 1) << bits) + (pivot & (NB - 1))
    mine = (pivot >> bits & (grid_rows - 1)) == lax.axis_index("row")
    return jnp.where(mine, local, -1)


def halves(x):
    high = x.astype(jnp.bfloat16)
    return high, (x - high.astype(jnp.float32)).astype(jnp.bfloat16)


def dot_pair(a, b):
    return lax.dot_general(
        a, b, (((1,), (0,)), ((), ())), preferred_element_type=jnp.float32
    )


def dot(a, b):
    high, rest = halves(a)
    b_high, b_rest = halves(b)
    both = jnp.concatenate([high, rest], axis=1)
    return dot_pair(both, jnp.concatenate([b_high, b_high], axis=0)) + dot_pair(high, b_rest)


def spread(block, lane):
    return jnp.broadcast_to(block[:, lane : lane + 1], block.shape)


def line(block, row):
    return jnp.broadcast_to(block[row : row + 1, :], block.shape)


def factor(a_ref, lu_ref, linv_ref, uinv_ref):
    n = TOP // SUB
    chunk = a_ref.shape[1] // 2
    lane = lax.broadcasted_iota(jnp.int32, (SUB, TOP), 1)
    sub = lax.broadcasted_iota(jnp.int32, (SUB, TOP), 0)
    row_id = lax.broadcasted_iota(jnp.int32, (TOP, TOP), 0)
    lane_id = lax.broadcasted_iota(jnp.int32, (TOP, TOP), 1)
    rest = jnp.concatenate([a_ref[slot, :chunk] for slot in range(TOP // chunk)], axis=0)
    low_rest = jnp.where(row_id == lane_id, 1.0, 0.0).astype(jnp.float32)
    eye = [low_rest[SUB * i : SUB * (i + 1)] for i in range(n)]
    unit = [jnp.where(sub == j, 1.0, 0.0).astype(jnp.float32) for j in range(SUB)]
    upp = None
    weights = jnp.ones((SUB, TOP), jnp.float32)
    for b in range(n):
        first = SUB * b
        block, rest = rest[:SUB], rest[SUB:]
        low, low_rest = low_rest[:SUB], low_rest[SUB:]
        cols = [spread(block, first + j) for j in range(SUB)]
        weight, entry, a_line, low_line = [], [], [], []
        for k in range(SUB):
            weight.append(1.0 / line(cols[k], k))
            weights = jnp.where(lane == first + k, weight[k], weights)
            entry.append([line(cols[j], k) if j > k else None for j in range(SUB)])
            a_line.append(jnp.where(lane > first + k, line(block, k), 0.0))
            low_line.append(line(low, k))
            if k < SUB - 1:
                multiplier = jnp.where(sub > k, cols[k] * weight[k], 0.0)
                for j in range(k + 1, SUB):
                    cols[j] = cols[j] - multiplier * entry[k][j]
                block = block - multiplier * a_line[k]
                low = low - multiplier * low_line[k]
        lu_ref[first : first + SUB, :] = block
        linv_ref[first : first + SUB, :] = low

        def over(x, rows):
            return x[:1] if rows != SUB else x

        def multipliers(cols, rows):
            cols = list(cols)
            for k in range(SUB):
                cols[k] = cols[k] * over(weight[k], rows)
                for j in range(k + 1, SUB):
                    cols[j] = cols[j] - cols[k] * over(entry[k][j], rows)
            return cols

        rows = TOP - first - SUB
        if rows:
            part = multipliers([spread(rest, first + j) for j in range(SUB)], rows)
            for k in range(SUB):
                rest = rest - part[k] * over(a_line[k], rows)
                low_rest = low_rest - part[k] * over(low_line[k], rows)
        if upp is not None:
            part = multipliers([spread(upp, first + j) for j in range(SUB)], first)
            for k in range(SUB):
                upp = upp - part[k] * over(a_line[k], first)
        own = eye[b]
        part = multipliers(unit, SUB)
        for k in range(SUB):
            own = own - part[k] * a_line[k]
        upp = own if upp is None else jnp.concatenate([upp, own], axis=0)
    scale = weights[:1]
    packed = lu_ref[...]
    lu_ref[...] = jnp.where(row_id > lane_id, packed * scale, packed)
    uinv_ref[...] = upp * scale


def finish_kernel(
    pivot_ref,
    a_ref,
    panel_ref,
    leads_ref,
    news_ref,
    olds_ref,
    lu,
    linv,
    uinv,
    out_ref,
    a_buf,
    p_buf,
    news,
    olds,
    upper,
    solved,
    top_rows,
    in_sem,
    side_sem,
    out_sem,
):
    my_row = lax.axis_index("row")
    my_col = lax.axis_index("col")
    spare = a_buf.shape[0] - SUB
    rows = spare // CHUNKS
    copies = [
        pltpu.make_async_copy(
            a_ref.at[pl.ds(rows * i, rows)], a_buf.at[pl.ds(rows * i, rows)], in_sem.at[i]
        )
        for i in range(CHUNKS)
    ]
    news_copy = pltpu.make_async_copy(news_ref, news, side_sem.at[0])
    olds_copy = pltpu.make_async_copy(olds_ref, olds, side_sem.at[1])
    panel_copy = pltpu.make_async_copy(panel_ref, p_buf.at[pl.ds(0, spare)], side_sem.at[2])
    for copy in (news_copy, olds_copy, panel_copy):
        copy.start()
    for copy in copies:
        copy.start()
    news_copy.wait()
    upper[...] = dot(linv[...], news[...].reshape(upper.shape))
    solved[...] = dot(uinv[...], upper[...])
    holds = my_col < 2
    own_lanes = (lax.broadcasted_iota(jnp.int32, (TOP, TOP), 1) < NB) & holds
    inverse = uinv[...]
    own = jnp.where(my_col == 0, inverse, pltpu.roll(inverse, NB, 1))
    solved[:, :TOP] = jnp.where(own_lanes, -own, solved[:, :TOP])
    top = pl.ds(pl.multiple_of(jnp.minimum(my_row, 1) * NB, NB), NB)
    corner = lu[top, :]
    corner = jnp.where(my_col == 0, corner, pltpu.roll(corner, NB, 1))
    top_rows[...] = upper[top, :]
    top_rows[:, :TOP] = jnp.where(own_lanes[:NB], corner, top_rows[:, :TOP])
    high, rest = halves(solved[...])
    twice = jnp.concatenate([high, high], axis=0)
    olds_copy.wait()
    panel_copy.wait()
    for copy in copies:
        copy.wait()

    chunk = olds.shape[1]

    def place(slot, carry):
        for row in range(chunk):
            index = place_of(pivot_ref, slot * chunk + row)
            index = jnp.where(index < 0, spare, index)
            a_buf[pl.ds(index, 1), :] = olds[slot, row : row + 1, :]
            p_buf[pl.ds(index, 1), :] = leads_ref[slot, chunk + row : chunk + row + 1, :]
        return carry

    lax.fori_loop(0, TOP // chunk, place, 0)
    dropped = (lax.broadcasted_iota(jnp.int32, (rows, a_buf.shape[1]), 1) < NB) & holds
    outs = []
    for i in range(CHUNKS):
        part = pl.ds(rows * i, rows)
        kept = jnp.where(dropped, 0.0, a_buf[part, :])
        left, left_rest = halves(p_buf[part, :])
        product = dot_pair(jnp.concatenate([left, left_rest], axis=1), twice)
        a_buf[part, :] = kept - (product + dot_pair(left, rest))
        if i == 0:

            @pl.when(my_row < 2)
            def _():
                a_buf[:NB, :] = top_rows[...]

        out = pltpu.make_async_copy(a_buf.at[part], out_ref.at[part], out_sem.at[i])
        out.start()
        outs.append(out)
    for out in outs:
        out.wait()


def finish(matrix, panel, leads, news, olds, lu, linv, uinv, pivots):
    any_spec = pl.BlockSpec(memory_space=pl.ANY)
    vmem = pl.BlockSpec(memory_space=pltpu.VMEM)
    return pl.pallas_call(
        finish_kernel,
        out_shape=jax.ShapeDtypeStruct(matrix.shape, jnp.float32),
        in_specs=[pl.BlockSpec(memory_space=pltpu.SMEM)]
        + [any_spec, any_spec, vmem, any_spec, any_spec, vmem, vmem, vmem],
        out_specs=any_spec,
        scratch_shapes=[
            pltpu.VMEM((matrix.shape[0] + SUB, matrix.shape[1]), jnp.float32),
            pltpu.VMEM((panel.shape[0] + SUB, TOP), jnp.float32),
            pltpu.VMEM(news.shape, jnp.float32),
            pltpu.VMEM(olds.shape, jnp.float32),
            pltpu.VMEM((TOP, matrix.shape[1]), jnp.float32),
            pltpu.VMEM((TOP, matrix.shape[1]), jnp.float32),
            pltpu.VMEM((NB, matrix.shape[1]), jnp.float32),
            pltpu.SemaphoreType.DMA((CHUNKS,)),
            pltpu.SemaphoreType.DMA((3,)),
            pltpu.SemaphoreType.DMA((CHUNKS,)),
        ],
        name="finish",
    )(pivots, matrix, panel, leads, news, olds, lu, linv, uinv)


def move_kernel(
    pivot_ref,
    a_ref,
    panel_ref,
    leads_ref,
    news_ref,
    olds_ref,
    lu_ref,
    linv_ref,
    uinv_ref,
    a_buf,
    lead_buf,
    picked_lead,
    pack,
    picked,
    parts,
    news,
    olds,
    tiles,
    tile_parts,
    tile_pair,
    leads,
    sums,
    panel,
    load_sem,
    slice_send,
    slice_recv,
    spread_send,
    pair_send,
    pair_recv,
    part_send,
    part_recv,
    top_send,
    top_recv,
    new_send,
    new_recv,
    old_send,
    old_recv,
    tile_send,
    tile_recv,
    fan_send,
    fan_recv,
    lead_send,
    lead_recv,
    panel_out,
    side_out,
):
    rows_dev = lax.axis_size("row")
    cols_dev = lax.axis_size("col")
    chips = cols_dev // 2
    my_row = lax.axis_index("row")
    my_col = lax.axis_index("col")
    chip = my_col // 2
    core = my_col % 2
    chunk = TOP // rows_dev
    half_rows = a_buf.shape[0] // 2
    slice_rows = half_rows // chips

    load_lead = pltpu.make_async_copy(a_ref.at[:, pl.ds(0, TOP)], lead_buf, load_sem.at[0])
    load = pltpu.make_async_copy(a_ref, a_buf, load_sem.at[1])

    @pl.when(chip == 0)
    def _():
        load_lead.start()

    load.start()
    barrier = pltpu.get_barrier_semaphore()
    for j in range(1, rows_dev):
        pl.semaphore_signal(
            barrier, inc=1, device_id={"row": lax.rem(my_row + j, rows_dev)}, device_id_type=MESH
        )
    for j in range(1, cols_dev):
        pl.semaphore_signal(
            barrier, inc=1, device_id={"col": lax.rem(my_col + j, cols_dev)}, device_id_type=MESH
        )

    def pick(table, target):
        def body(step, carry):
            for j in range(PLACES):
                k = step * PLACES + j
                index = place_of(pivot_ref, k)
                row = table[pl.ds(jnp.maximum(index, 0), 1), :]
                target[pl.ds(k, 1), :] = jnp.where(index >= 0, row, 0.0)
            return carry

        lax.fori_loop(0, TOP // PLACES, body, 0)

    first = lax.broadcasted_iota(jnp.int32, (slice_rows, TOP), 1) < NB
    first_tile = lax.broadcasted_iota(jnp.int32, (chunk, TOP), 1) < NB

    def top_start(d):
        return d * chunk - d * chunk // NB * NB

    @pl.when(chip == 0)
    def _():
        load_lead.wait()
        pick(lead_buf, picked_lead)
        for d in range(rows_dev):
            start = top_start(d)
            top = pltpu.roll(lead_buf[start : start + chunk, :], NB, 1)
            top = jnp.where(my_row == d * chunk // NB, top, 0.0)
            tiles[d] = jnp.where(first_tile, picked_lead[chunk * d : chunk * (d + 1), :], top)

    @pl.when(chip != 0)
    def _():
        load.wait()
        pick(a_buf, picked)

    pl.semaphore_wait(barrier, rows_dev + cols_dev - 2)

    def to_row(source, target, send, recv, d):
        return pltpu.make_async_remote_copy(
            src_ref=source,
            dst_ref=target,
            send_sem=send,
            recv_sem=recv,
            device_id={"row": d},
            device_id_type=MESH,
        )

    def to_col(source, target, send, recv, q):
        return pltpu.make_async_remote_copy(
            src_ref=source,
            dst_ref=target,
            send_sem=send,
            recv_sem=recv,
            device_id={"col": q},
            device_id_type=MESH,
        )

    def other(j):
        return lax.rem(my_row + j, rows_dev)

    def tile_copy(j):
        d = other(j)
        return to_row(
            tiles.at[d], tile_parts.at[my_row], tile_send.at[j], tile_recv.at[my_row], d
        )

    def slice_copy(s, t, send):
        return to_col(pack.at[core, s], pack.at[core, s], send, slice_recv.at[s], t * 2 + core)

    half = chunk // 2
    all_rows = pl.ds(0, chunk)

    def part_of(d, part=None):
        start, size = (0, chunk) if part is None else (part * half, half)
        return picked.at[pl.ds(d * chunk + start, size)]

    def part_copy(slot, target, relay, part=None):
        rows = all_rows if part is None else pl.ds(part * half, half)
        return to_row(
            part_of(other(target), part),
            parts.at[slot, rows],
            part_send.at[slot],
            part_recv.at[slot],
            other(relay),
        )

    def part_copies():
        return [
            part_copy(0, 7, 1),
            part_copy(1, 5, 7),
            part_copy(2, 4, 6, 0),
            part_copy(3, 1, 7),
            part_copy(4, 3, 1),
            part_copy(5, 4, 2, 1),
        ]

    def sum_copy(which, target):
        slot = 6 + which
        return to_row(
            sums.at[which], parts.at[slot], part_send.at[slot], part_recv.at[slot], other(target)
        )

    def value_of(d):
        return picked[pl.ds(pl.multiple_of(d * chunk, chunk), chunk), :]

    def top_copy(d):
        return to_row(
            a_buf.at[pl.ds(top_start(d), chunk), :], olds.at[d], top_send.at[d], top_recv, d
        )

    def ring_copy(j, table, send, recv):
        return to_row(table.at[my_row], table.at[my_row], send.at[j], recv.at[my_row], other(j))

    def arrive(j, table, send, recv):
        s = other(j)
        to_row(table.at[s], table.at[s], send.at[j], recv.at[s], s).wait_recv()

    def hop(table, slot, part, d, send, recv):
        return to_row(table.at[slot, part], table.at[slot, part], send, recv, d)

    def stage_one(table, send, recv):
        return [
            hop(table, my_row, all_rows, other(j), send.at[j], recv.at[my_row]) for j in (2, 6)
        ]

    def stage_two(table, send, recv):
        below, above = other(6), other(2)
        upper = pl.ds(0, half)
        lower = pl.ds(half, half)
        return [
            hop(table, below, all_rows, other(7), send.at[0], recv.at[below]),
            hop(table, below, all_rows, other(1), send.at[1], recv.at[below]),
            hop(table, below, upper, other(2), send.at[3], recv.at[below]),
            hop(table, above, all_rows, other(1), send.at[4], recv.at[above]),
            hop(table, above, all_rows, other(7), send.at[5], recv.at[above]),
            hop(table, above, lower, other(6), send.at[7], recv.at[rows_dev]),
        ]

    def begin(table, send, recv):
        for copy in stage_one(table, send, recv):
            copy.start()

    def forward(table, send, recv):
        arrive(6, table, send, recv)
        arrive(2, table, send, recv)
        for copy in stage_two(table, send, recv):
            copy.start()

    def gathered(table, send, recv):
        for j in (1, 3, 5, 7):
            arrive(j, table, send, recv)
        far = other(4)
        hop(table, far, pl.ds(0, half), far, send.at[0], recv.at[far]).wait_recv()
        hop(table, far, pl.ds(half, half), far, send.at[0], recv.at[rows_dev]).wait_recv()

    def sent(table, send, recv):
        for copy in stage_one(table, send, recv) + stage_two(table, send, recv):
            copy.wait_send()

    def fan_copy(j):
        q = lax.rem(my_col + j, cols_dev)
        return to_col(
            tile_pair.at[core], tile_pair.at[core], fan_send.at[j], fan_recv.at[core], q
        )

    @pl.when(chip == 0)
    def _():
        for j in range(1, rows_dev):
            tile_copy(j).start()
        tile_parts[my_row] = tiles[my_row]
        for s in range(chips):
            low = lead_buf[slice_rows * s : slice_rows * (s + 1), :]
            high = lead_buf[half_rows + slice_rows * s : half_rows + slice_rows * (s + 1), :]
            at_zero = jnp.where(core == 0, low, high)
            shifted = jnp.where(core == 0, high, low)
            pack[core, s] = jnp.where(first, at_zero, pltpu.roll(shifted, NB, 1))
        for s in range(1, chips):
            slice_copy(s, s, slice_send.at[s]).start()
        load.wait()
        pick(a_buf, picked)

    for copy in part_copies():
        copy.start()
    for d in range(rows_dev):
        owner = d * chunk // NB

        @pl.when(my_row == owner)
        def _():
            if d == owner:
                olds[d] = a_buf[top_start(d) : top_start(d) + chunk, :]
            else:
                top_copy(d).start()

    @pl.when(chip == 0)
    def _():
        for j in range(1, rows_dev):
            arrive(j, tile_parts, tile_send, tile_recv)
        total = tile_parts[0]
        for s in range(1, rows_dev):
            total = total + tile_parts[s]
        tile_pair[core] = total
        for j in range(1, cols_dev):
            fan_copy(j).start()

    @pl.when(chip != 0)
    def _():
        slice_copy(chip, chip, slice_send.at[0]).wait_recv()

    for j in range(1, chips):
        t = lax.rem(chip + j, chips)

        @pl.when(t != 0)
        def _():
            slice_copy(chip, t, spread_send.at[j]).start()

    for d in range(rows_dev):
        if d != d * chunk // NB:

            @pl.when(my_row == d)
            def _():
                top_copy(d).wait_recv()

    begin(olds, old_send, old_recv)
    for copy in part_copies():
        copy.wait_recv()
    low_sum = value_of(other(6)) + parts[0] + parts[1]
    sums[0, :half] = low_sum[:half] + parts[2, :half]
    sums[0, half:] = low_sum[half:]
    high_sum = value_of(other(2)) + parts[3] + parts[4]
    sums[1, :half] = high_sum[:half]
    sums[1, half:] = high_sum[half:] + parts[5, half:]
    sum_copy(0, 6).start()
    sum_copy(1, 2).start()
    forward(olds, old_send, old_recv)
    sum_copy(0, 6).wait_recv()
    sum_copy(1, 2).wait_recv()
    news[my_row] = value_of(my_row) + parts[6] + parts[7]
    begin(news, new_send, new_recv)

    for c in range(2):

        @pl.when(my_col != c)
        def _():
            to_col(
                tile_pair.at[c], tile_pair.at[c], fan_send.at[0], fan_recv.at[c], c
            ).wait_recv()

    zero_tile = tile_pair[0]
    one_tile = tile_pair[1]
    leads[my_row, :chunk] = jnp.where(first_tile, zero_tile, pltpu.roll(one_tile, NB, 1))
    leads[my_row, chunk:] = jnp.where(first_tile, pltpu.roll(zero_tile, NB, 1), one_tile)
    for j in range(1, rows_dev):
        ring_copy(j, leads, lead_send, lead_recv).start()
    forward(news, new_send, new_recv)

    groups = min(4, chips)
    per = chips // groups

    def panel_copies(g):
        size = per * slice_rows
        copies = []
        for side in range(2):
            rows = pl.ds(side * half_rows + g * size, size)
            copies.append(
                pltpu.make_async_copy(panel.at[rows], panel_ref.at[rows], panel_out.at[2 * g + side])
            )
        return copies

    def pair_copy(g, which):
        held = pack.at[which, pl.ds(g * per, per)]
        return to_col(held, held, pair_send.at[g], pair_recv.at[g], chip * 2 + 1 - core)

    for g in range(groups):

        @pl.when(chip != 0)
        def _():
            for s in range(g * per, (g + 1) * per):

                @pl.when(chip != s)
                def _():
                    slice_copy(s, chip, slice_send.at[0]).wait_recv()

        pair_copy(g, core).start()

    for g in range(groups):
        pair_copy(g, 1 - core).wait_recv()
        for s in range(g * per, (g + 1) * per):
            zero_pack = pack[0, s]
            one_pack = pack[1, s]
            low = slice(slice_rows * s, slice_rows * (s + 1))
            high = slice(half_rows + slice_rows * s, half_rows + slice_rows * (s + 1))
            panel[low, :] = jnp.where(first, zero_pack, one_pack)
            panel[high, :] = pltpu.roll(jnp.where(first, one_pack, zero_pack), NB, 1)
        for copy in panel_copies(g):
            copy.start()

    for j in range(1, rows_dev):
        arrive(j, leads, lead_send, lead_recv)
    factor(leads, lu_ref, linv_ref, uinv_ref)

    side = [
        pltpu.make_async_copy(table, target, side_out.at[i])
        for i, (table, target) in enumerate(
            ((leads, leads_ref), (news, news_ref), (olds, olds_ref))
        )
    ]
    side[0].start()
    gathered(olds, old_send, old_recv)
    side[2].start()
    gathered(news, new_send, new_recv)
    side[1].start()

    for copy in part_copies():
        copy.wait_send()
    sum_copy(0, 6).wait_send()
    sum_copy(1, 2).wait_send()
    for j in range(1, rows_dev):
        ring_copy(j, leads, lead_send, lead_recv).wait_send()
    sent(news, new_send, new_recv)
    sent(olds, old_send, old_recv)
    for d in range(rows_dev):
        owner = d * chunk // NB
        if d != owner:

            @pl.when(my_row == owner)
            def _():
                top_copy(d).wait_send()

    @pl.when(chip == 0)
    def _():
        for j in range(1, rows_dev):
            tile_copy(j).wait_send()
        for s in range(1, chips):
            slice_copy(s, s, slice_send.at[s]).wait_send()
        for j in range(1, cols_dev):
            fan_copy(j).wait_send()

    for j in range(1, chips):
        t = lax.rem(chip + j, chips)

        @pl.when(t != 0)
        def _():
            slice_copy(chip, t, spread_send.at[j]).wait_send()

    for g in range(groups):
        pair_copy(g, core).wait_send()
        for copy in panel_copies(g):
            copy.wait()
    for copy in side:
        copy.wait()


def move(matrix, pivots):
    rows_dev = lax.axis_size("row")
    cols_dev = lax.axis_size("col")
    chips = cols_dev // 2
    chunk = TOP // rows_dev
    rows, cols = matrix.shape
    dma = pltpu.SemaphoreType.DMA
    f32 = jnp.float32
    by_row = dma((rows_dev,))
    by_chip = dma((chips,))
    return pl.pallas_call(
        move_kernel,
        out_shape=[
            jax.ShapeDtypeStruct((rows, TOP), f32),
            jax.ShapeDtypeStruct((rows_dev, 2 * chunk, TOP), f32),
            jax.ShapeDtypeStruct((rows_dev, chunk, cols), f32),
            jax.ShapeDtypeStruct((rows_dev, chunk, cols), f32),
            *[jax.ShapeDtypeStruct((TOP, TOP), f32)] * 3,
        ],
        in_specs=[
            pl.BlockSpec(memory_space=pltpu.SMEM),
            pl.BlockSpec(memory_space=pl.ANY),
        ],
        out_specs=[pl.BlockSpec(memory_space=pl.ANY)] * 4
        + [pl.BlockSpec(memory_space=pltpu.VMEM)] * 3,
        scratch_shapes=[
            pltpu.VMEM((rows, cols), f32),
            pltpu.VMEM((rows, TOP), f32),
            pltpu.VMEM((TOP, TOP), f32),
            pltpu.VMEM((2, chips, rows // 2 // chips, TOP), f32),
            pltpu.VMEM((TOP, cols), f32),
            pltpu.VMEM((rows_dev, chunk, cols), f32),
            pltpu.VMEM((rows_dev, chunk, cols), f32),
            pltpu.VMEM((rows_dev, chunk, cols), f32),
            pltpu.VMEM((rows_dev, chunk, TOP), f32),
            pltpu.VMEM((rows_dev, chunk, TOP), f32),
            pltpu.VMEM((2, chunk, TOP), f32),
            pltpu.VMEM((rows_dev, 2 * chunk, TOP), f32),
            pltpu.VMEM((2, chunk, cols), f32),
            pltpu.VMEM((rows, TOP), f32),
            dma((2,)),
            by_chip,
            by_chip,
            by_chip,
            dma((4,)),
            dma((4,)),
            by_row,
            by_row,
            by_row,
            dma,
            by_row,
            dma((rows_dev + 1,)),
            by_row,
            dma((rows_dev + 1,)),
            by_row,
            by_row,
            dma((cols_dev,)),
            dma((2,)),
            by_row,
            by_row,
            dma((8,)),
            dma((3,)),
        ],
        compiler_params=pltpu.CompilerParams(collective_id=0, has_side_effects=True),
        name="move",
    )(pivots, matrix)


def shards(matrix, pivots):
    panel, leads, news, olds, lu, linv, uinv = move(matrix, pivots)
    return finish(matrix, panel, leads, news, olds, lu, linv, uinv, pivots)


def solution(mesh):
    placed = (P("row", "col"), P())
    return jax.shard_map(
        shards, mesh=mesh, in_specs=placed, out_specs=P("row", "col"), check_vma=False
    )
```
